32 devices in a mesh: boson: 8 (over z, x), block: 4 (over y, core).
Axes of the slice: x: 2, y: 2, z: 4, core: 2. Of those that a mesh axis runs over, the one named last changes fastest.
Arguments:
- gamma_ph: bfloat16 [32, 1024, 1024], P('boson', 'block'), may hold values from -6 to 6
- full_ph: bfloat16 [32, 1024, 1024], P('boson', 'block'), may hold values from -0.1875 to 0.1875
- chi_ph: float32 [32, 1024], P('boson'), may hold values from 0.3 to 3
- pp_vertex: bfloat16 [32, 1024, 1024], P('boson', 'block'), may hold values from -0.1875 to 0.1875
- chi_pp: float32 [32, 1024], P('boson'), may hold values from 0.3 to 3
- relabel: int32 [32, 16, 8], replicated, may hold values from 0 to 31, as said below
Outputs:
- vertex_new: bfloat16 [32, 1024, 1024], P('boson', 'block')
The draws below stay inside these ranges and needn't reach their ends.
Inputs may be any that keep to these rules, and one draw needn't show every extreme that they name: `relabel`: for each row tile and column block the table is a permutation of the 32 points. The owner of the target point (target // 4) is the source's owner (q // 4) plus a shift modulo 8, and both this shift and the target's position among its owner's points (target % 4) depend only on the row tile, the column block and q % 4. Row tiles b * 4 to (b + 1) * 4 - 1 form row block b; within one row block, at most 17 of the 128 triples of position, row tile and column block share a shift, and some shift is shared by exactly 17; in every row block the shifts 1, 4 and 7 each occur.
All inputs are finite; a program needn't handle non-finite values.
Results may differ from the reference program's by a relative error of at most 0.0063.
Values may be sent and summed in bfloat16 or wider, within the bound.
A program may use at most 128 MiB of HBM per device.

```python
import math
import jax
import jax.numpy as jnp
from jax import lax

M = 1024
CB = 8
RS = 4
RB = 16
QD = 4
QB = 32
CAP = 17
N_BOSON = 8
N_BLOCK = 4


def draw_relabel(key, part):
    item_total = QD * RS * CB
    blocks = []
    values = jnp.arange(N_BOSON, dtype=jnp.int32)
    for row_block in range(N_BLOCK):
        block_key = jax.random.fold_in(key, 101 + row_block)
        key_offset, key_mix, key_slot = jax.random.split(block_key, 3)
        ranks = jax.random.permutation(key_offset, N_BOSON).astype(jnp.int32) + 3
        ranks = jnp.where(values == 1, 0, ranks)
        ranks = jnp.where(values == N_BOSON // 2, 1, ranks)
        ranks = jnp.where(values == N_BOSON - 1, 2, ranks)
        shuffled = jnp.argsort(ranks, stable=True).astype(jnp.int32)
        spread = shuffled[jnp.arange(item_total) // CAP]
        spread = spread[jax.random.permutation(key_mix, item_total)].reshape(QD, RS * CB)
        position = jax.vmap(lambda subkey: jax.random.permutation(subkey, QD))(jax.random.split(key_slot, RS * CB)).T
        source = jnp.arange(N_BOSON, dtype=jnp.int32)[:, None, None]
        target_point = (source + spread[None]) % N_BOSON * QD + position[None]
        blocks.append(target_point.reshape(N_BOSON * QD, RS, CB).astype(jnp.int32))
    return jnp.stack(blocks, axis=1).reshape(N_BOSON * QD, RS * N_BLOCK, CB)


def steps_of(key, shape, cuts, smallest, top_value):
    factor_of = 1.0
    for dim, parts in cuts:
        heights = jax.random.uniform(jax.random.fold_in(jax.random.fold_in(key, 6), dim), (parts,), jnp.float32, smallest / len(cuts), top_value / len(cuts))
        factor_of = factor_of * jnp.repeat(jnp.exp(heights), shape[dim] // parts).reshape((-1,) + (1,) * (len(shape) - 1 - dim))
    return factor_of


def scatter_about(key, extent, deviation, reach, cuts=(), kind=jnp.bfloat16):
    array = jax.random.normal(key, extent, jnp.float32) * deviation
    if len(cuts) > 0:
        array = steps_of(key, extent, cuts, -0.22, 0.18) * array
    return jnp.clip(array, min=-reach, max=reach).astype(kind)


def setup_inputs(seed: int = 0) -> dict:
    arg_keys = jax.random.split(jax.random.key(seed), 7)
    gamma_ph = scatter_about(arg_keys[0], (QB, M, M), 1.0, 6.0, ((0, 8), (1, 4)))
    full_ph = scatter_about(arg_keys[1], (QB, M, M), M ** -0.5, 0.1875, ((0, 8), (1, 4)))
    chi_ph = jnp.clip(jnp.exp(math.log(3.0) - 2.3025851 * jax.random.uniform(arg_keys[2], (QB, M), jnp.float32) ** steps_of(arg_keys[2], (QB, M), ((0, 8),), -0.2, 0.2)), 0.3, 3.0)
    pp_vertex = scatter_about(arg_keys[3], (QB, M, M), M ** -0.5, 0.1875, ((0, 8), (1, 4)))
    chi_pp = jnp.clip(jnp.exp(math.log(3.0) - 2.3025851 * jax.random.uniform(arg_keys[4], (QB, M), jnp.float32) ** steps_of(arg_keys[4], (QB, M), ((0, 8),), -0.2, 0.2)), 0.3, 3.0)
    relabel = draw_relabel(jax.random.fold_in(arg_keys[6], 71), 0)
    return {"gamma_ph": gamma_ph, "full_ph": full_ph, "chi_ph": chi_ph, "pp_vertex": pp_vertex, "chi_pp": chi_pp, "relabel": relabel}


def to_tiles(matrix):
    return matrix.reshape(QB, RB, M // RB, CB, M // CB).transpose(0, 1, 3, 2, 4)


def from_tiles(tile_stack):
    return tile_stack.transpose(0, 1, 3, 2, 4).reshape(QB, M, M)


def bubble_product(left_side, column_scale, right_side):
    def single(inputs):
        left_one, scale_one, right_one = inputs
        scaled = (left_one.astype(jnp.float32) * scale_one[None, :]).astype(jnp.bfloat16)
        return jnp.dot(scaled, right_one, preferred_element_type=jnp.float32)
    return lax.map(single, (left_side, column_scale, right_side))


def reference(gamma_ph, full_ph, chi_ph, pp_vertex, chi_pp, relabel):
    phi_ph = bubble_product(gamma_ph, chi_ph, full_ph)
    ph_tiles = to_tiles(phi_ph.astype(jnp.bfloat16))
    row_index = jnp.broadcast_to(jnp.arange(RB, dtype=jnp.int32)[None, :, None], relabel.shape)
    col_index = jnp.broadcast_to(jnp.arange(CB, dtype=jnp.int32)[None, None, :], relabel.shape)
    pp_tiles = jnp.zeros_like(ph_tiles).at[relabel, row_index, col_index].set(ph_tiles)
    relabelled = from_tiles(pp_tiles)
    phi_pp = bubble_product(relabelled, chi_pp, pp_vertex).astype(jnp.bfloat16)
    returned = to_tiles(phi_pp)[relabel, row_index, col_index]
    vertex_new = gamma_ph.astype(jnp.float32) + phi_ph + from_tiles(returned).astype(jnp.float32)
    return vertex_new.astype(jnp.bfloat16)
```

```python
import functools
import jax
import jax.numpy as jnp
from jax import lax
from jax.experimental import pallas as pl
from jax.experimental.pallas import tpu as pltpu
from jax.sharding import PartitionSpec as P

MESH = pl.DeviceIdType.MESH
DMA = pltpu.SemaphoreType.DMA
PARTS = 4
LANES = 128


def loop(start, stop, body):
    lax.fori_loop(start, stop, lambda i, carry: (body(i), carry)[1], 0)


class Schedule:
    def __init__(self, chunks, capacity, lag, first=0):
        self.chunks, self.capacity, self.lag, self.first = chunks, capacity, lag, first
        self.start = max(lag, 0)
        self.early = chunks - self.start
        assert self.sent(chunks - 1) < capacity

    def sent(self, g):
        return 0 if g < self.start else g + 1 - self.start + self.first

    def due(self, g):
        return jnp.where(g < self.start, 0, g + 1 - self.start + self.first)


class Gather:
    def __init__(self, nblock, shard, whole, sems):
        self.nblock, self.shard, self.whole = nblock, shard, whole
        self.far_s, self.far_r, self.near_s, self.near_r, self.fwd_s, self.fwd_r, self.loc = sems
        self.points, self.rows, order = shard.shape
        self.cols = order // PARTS
        self.chunks = self.points * PARTS
        self.boson = lax.axis_index("boson")
        self.here = lax.axis_index("block")
        self.partner = self.here + 1 - 2 * (self.here % 2)

    def peers(self):
        out = [self.partner]
        for j in range(1, self.nblock // 2):
            out.append((self.here + 2 * j) % self.nblock)
        return out

    def columns(self, g):
        return pl.ds(pl.multiple_of(g % PARTS * self.cols, self.cols), self.cols)

    def source(self, g):
        return self.shard.at[g // PARTS, :, self.columns(g)]

    def place(self, g, owner):
        rows = pl.ds(pl.multiple_of(owner * self.rows, self.rows), self.rows)
        return self.whole.at[g // PARTS, rows, self.columns(g)]

    def far(self, g, j, owner):
        return pltpu.make_async_remote_copy(
            src_ref=self.source(g), dst_ref=self.place(g, owner),
            send_sem=self.far_s.at[j - 1, g], recv_sem=self.far_r.at[j - 1, g],
            device_id=(self.boson, (self.here + 2 * j) % self.nblock), device_id_type=MESH)

    def near(self, g, owner):
        return pltpu.make_async_remote_copy(
            src_ref=self.source(g), dst_ref=self.place(g, owner),
            send_sem=self.near_s.at[g], recv_sem=self.near_r.at[g],
            device_id=(self.boson, self.partner), device_id_type=MESH)

    def forward(self, g, j, owner):
        return pltpu.make_async_remote_copy(
            src_ref=self.place(g, owner), dst_ref=self.place(g, owner),
            send_sem=self.fwd_s.at[j - 1, g], recv_sem=self.fwd_r.at[j - 1, g],
            device_id=(self.boson, self.partner), device_id_type=MESH)

    def own(self):
        rows = pl.ds(pl.multiple_of(self.here * self.rows, self.rows), self.rows)
        return pltpu.make_async_copy(self.shard, self.whole.at[:, rows], self.loc)

    def each_far(self, act):
        for j in range(1, self.nblock // 2):
            act(j)

    def start(self):
        def one(g):
            self.each_far(lambda j: self.far(g, j, self.here).start())
            self.near(g, self.here).start()
        loop(0, self.chunks, one)

    def relay(self, g):
        def one(j):
            owner = (self.here + self.nblock - 2 * j) % self.nblock
            self.far(g, j, owner).wait_recv()
            self.forward(g, j, owner).start()
        self.each_far(one)

    def arrived(self, g):
        self.near(g, self.partner).wait_recv()
        def one(j):
            twin = (self.partner + self.nblock - 2 * j) % self.nblock
            self.forward(g, j, twin).wait_recv()
        self.each_far(one)

    def sent_far(self):
        loop(0, self.chunks,
             lambda g: self.each_far(lambda j: self.far(g, j, self.here).wait_send()))

    def sent_near(self):
        def one(g):
            self.near(g, self.here).wait_send()
            def fwd(j):
                owner = (self.here + self.nblock - 2 * j) % self.nblock
                self.forward(g, j, owner).wait_send()
            self.each_far(fwd)
        loop(0, self.chunks, one)


def gather_scratch(nblock, points):
    far, chunks = max(nblock // 2 - 1, 1), points * PARTS
    return [DMA((far, chunks)), DMA((far, chunks)), DMA((chunks,)), DMA((chunks,)),
            DMA((far, chunks)), DMA((far, chunks)), DMA]


class Exchange:
    def __init__(self, nboson, outgoing, incoming, send, recv):
        self.n, self.outgoing, self.incoming = nboson, outgoing, incoming
        self.send, self.recv = send, recv
        self.capacity = outgoing.shape[1]
        self.boson = lax.axis_index("boson")
        self.block = lax.axis_index("block")

    def peers(self):
        return [(self.boson + s) % self.n for s in range(1, self.n)]

    def shift(self, i):
        return self.n // 2 + (1 - 2 * (i % 2)) * ((i + 1) // 2)

    def copy(self, s, slot, start=0, size=None):
        dest = (self.boson + s) % self.n
        slots = pl.ds(start, self.capacity if size is None else size)
        return pltpu.make_async_remote_copy(
            src_ref=self.outgoing.at[dest, slots], dst_ref=self.incoming.at[slot, slots],
            send_sem=self.send.at[s], recv_sem=self.recv.at[s],
            device_id=(dest, self.block), device_id_type=MESH)

    def pack(self, target, dest, tiles, table, start, size):
        for k in range(size):
            target[dest, start + k] = tiles[table[dest * self.capacity + start + k]]

    def part(self, tiles, table, start, size):
        def pack(i):
            dest = (self.boson + self.shift(i)) % self.n
            self.pack(self.outgoing, dest, tiles, table, start, size)
        def send(i):
            self.copy(self.shift(i), self.boson, start, size).start()
        pack(0)
        def one(i):
            pack(i)
            send(i - 1)
        loop(1, self.n - 1, one)
        return lambda: send(self.n - 2)

    def keep(self, tiles, table):
        self.pack(self.incoming, self.boson, tiles, table, 0, self.capacity)

    def received(self):
        loop(1, self.n, lambda s: self.copy(s, (self.boson + self.n - s) % self.n).wait_recv())

    def sent(self):
        loop(1, self.n, lambda s: self.copy(s, self.boson).wait_send())


def greet(block_peers, boson_peers):
    barrier = pltpu.get_barrier_semaphore()
    boson, block = lax.axis_index("boson"), lax.axis_index("block")
    for peer in block_peers:
        pl.semaphore_signal(barrier, inc=1, device_id=(boson, peer), device_id_type=MESH)
    for peer in boson_peers:
        pl.semaphore_signal(barrier, inc=1, device_id=(peer, block), device_id_type=MESH)
    pl.semaphore_wait(barrier, len(block_peers) + len(boson_peers))


def own_targets(nboson, targets, first_row, row_tiles):
    _, col_blocks, count = targets.shape
    points, per_point = count // nboson, row_tiles * col_blocks
    boson = lax.axis_index("boson")
    flat = targets[pl.ds(first_row, row_tiles)].reshape(per_point, count)
    lane = lax.broadcasted_iota(jnp.int32, flat.shape, 1)
    return jnp.concatenate(
        [jnp.sum(jnp.where(lane == boson * points + q, flat, 0), axis=1, keepdims=True)
         for q in range(points)], axis=0)


def decode(nboson, points, col_blocks, per_point, own):
    total = points * per_point
    boson = lax.axis_index("boson")
    item = lax.broadcasted_iota(jnp.int32, (total, 1), 0)
    shift = ((own >> (points.bit_length() - 1)) - boson) & (nboson - 1)
    target = (own & (points - 1)) * per_point + (item & (per_point - 1))
    def chunk(place):
        wide = col_blocks // PARTS
        column = place & (col_blocks - 1)
        return (place >> (per_point.bit_length() - 1)) * PARTS + (column >> (wide.bit_length() - 1))
    return item, shift, target, chunk(item), chunk(target)


def slot_tables(nboson, capacity, targets, row_tiles, rows):
    _, col_blocks, count = targets.shape
    points, per_point = count // nboson, row_tiles * col_blocks
    total = points * per_point
    boson = lax.axis_index("boson")
    own = own_targets(nboson, targets, lax.axis_index("block") * row_tiles, row_tiles)
    item, shift, target, ahead, home = decode(nboson, points, col_blocks, per_point, own)

    def spread(keys, values, width):
        wanted = lax.broadcasted_iota(jnp.int32, (total, width), 1)
        return jnp.sum(jnp.where(keys == wanted, values, 0), axis=0, keepdims=True)

    same = spread(item, shift, total) == shift
    def rank(key):
        earlier = same & (spread(item, key, total) < key)
        return jnp.sum(jnp.where(earlier, 1, 0), axis=1, keepdims=True)

    there = ((boson + shift) & (nboson - 1)) * capacity
    here = ((boson - shift) & (nboson - 1)) * capacity
    out_rank, back_rank = rank(ahead * total + item), rank(home * total + target)
    width = rows.shape[0] // 8 * rows.shape[1]
    last_slot, last_item = nboson * capacity - 1, total - 1
    for k, (keys, values, last) in enumerate((
            (item, there + back_rank, last_slot), (there + out_rank, item, last_item),
            (target, here + out_rank, last_slot), (here + back_rank, target, last_item))):
        line = jnp.minimum(spread(keys, values, width), last)
        for h in range(width // LANES):
            rows[h * 8 + k:h * 8 + k + 1, :] = line[:, h * LANES:(h + 1) * LANES]


def late_tiles(nboson, targets, row_tiles, schedules):
    row_count, col_blocks, count = targets.shape
    points, per_point = count // nboson, row_tiles * col_blocks
    total, chunks = points * per_point, points * PARTS
    lane = lax.broadcasted_iota(jnp.int32, (total, chunks * nboson), 1)
    wanted, upto = lane & (nboson - 1), lane >> (nboson.bit_length() - 1)
    late = 0
    for b in range(row_count // row_tiles):
        own = own_targets(nboson, targets, b * row_tiles, row_tiles)
        _, shift, _, *arrivals = decode(nboson, points, col_blocks, per_point, own)
        match = shift == wanted
        number = jnp.sum(jnp.where(match, 1, 0), axis=0, keepdims=True)
        for arrival, schedule in zip(arrivals, schedules):
            ready = jnp.sum(jnp.where(match & (arrival <= upto), 1, 0), axis=0, keepdims=True)
            due = jnp.minimum(schedule.due(upto[0:1]), number)
            late = late + jnp.where((ready < due) & (wanted[0:1] > 0), 1, 0)
    return jnp.sum(late, axis=1, keepdims=True)


class Table:
    def __init__(self, ref, k):
        self.ref, self.k = ref, k

    def __getitem__(self, i):
        return self.ref[i // LANES * 8 + self.k, i % LANES]


def kernel(nboson, nblock, row_tiles, col_blocks, lag, *refs):
    relabel, gamma_in, full_in, chi_ph, pp_in, chi_pp, out, *refs = refs
    late, refs = (refs[0], refs[1:]) if lag is not None else (None, refs)
    (full, pp, gamma, scaled, base, tiles, packed, landed, back, returned,
     targets, table_rows, table,
     gamma_sem, table_sem, ahead_s, ahead_r, home_s, home_r, *gather_sems) = refs
    half = len(gather_sems) // 2
    first = Gather(nblock, full_in, full, gather_sems[:half])
    second = Gather(nblock, pp_in, pp, gather_sems[half:])
    ahead = Exchange(nboson, packed, landed, ahead_s, ahead_r)
    home = Exchange(nboson, back, returned, home_s, home_r)
    points, rows, order = gamma.shape
    chunks = first.chunks
    high, wide = rows // row_tiles, order // col_blocks
    capacity = landed.shape[1]
    send_slot, item_of, back_slot, back_item_of = (Table(table, i) for i in range(4))
    load_targets = pltpu.make_async_copy(relabel, targets, table_sem.at[0])
    load_table = pltpu.make_async_copy(table_rows, table, table_sem.at[1])
    load_gamma = pltpu.make_async_copy(gamma_in, gamma, gamma_sem)

    first.own().start()
    load_gamma.start()
    load_targets.start()
    second.own().start()
    greet(first.peers(), ahead.peers())
    first.start()

    load_gamma.wait()
    for q in range(points):
        scaled[q] = (gamma[q].astype(jnp.float32) * chi_ph[q:q + 1, :]).astype(jnp.bfloat16)
    load_targets.wait()
    slot_tables(nboson, capacity, targets, row_tiles, table_rows)
    load_table.start()
    if lag is None:
        ahead_plan = home_plan = None
    else:
        ahead_plan = Schedule(chunks, capacity, lag)
        home_plan = Schedule(chunks, capacity, chunks // 2 - 1, 1)
        late[...] = jnp.broadcast_to(
            late_tiles(nboson, targets, row_tiles, (ahead_plan, home_plan)), late.shape)
    first.own().wait()
    load_table.wait()

    def cut(wire, g):
        q, column = g // PARTS, g % PARTS * (first.cols // wide)
        for r in range(row_tiles):
            for k in range(first.cols // wide):
                item = (q * row_tiles + r) * col_blocks + column + k
                tiles[item] = wire[r * high:(r + 1) * high, k * wide:(k + 1) * wide]

    def product(gather, g):
        q, at = g // PARTS, gather.columns(g)
        phi = jnp.dot(scaled[q], gather.whole[q, :, at], preferred_element_type=jnp.float32)
        cut(phi.astype(jnp.bfloat16), g)
        return q, at, phi

    def ph(g):
        first.arrived(g)
        q, at, phi = product(first, g)
        base[q, :, at] = gamma[q, :, at].astype(jnp.float32) + phi

    def staged(exchange, table, plan, begin, step):
        if plan is None:
            loop(begin, chunks, step)
            sent = 0
        else:
            loop(begin, plan.start, step)
            def one(g, size, slot):
                step(g)
                exchange.part(tiles, table, slot, size)()
            one(plan.start, 1 + plan.first, 0)
            loop(plan.start + 1, chunks, lambda g: one(g, 1, g - plan.start + plan.first))
            sent = plan.sent(chunks - 1)
        last = exchange.part(tiles, table, sent, capacity - sent)
        exchange.keep(tiles, table)
        last()

    def ahead_step(g):
        @pl.when(g + 1 < chunks)
        def _():
            first.relay(g + 1)
        @pl.when(g == chunks - 3)
        def _():
            second.start()
        ph(g)

    first.relay(0)
    staged(ahead, item_of, ahead_plan, 0, ahead_step)
    first.sent_far()
    first.sent_near()
    second.own().wait()
    loop(0, chunks // 2, second.relay)
    ahead.received()

    flat = landed.reshape(nboson * capacity, high, wide)
    def unpack(p):
        chi = chi_pp[pl.ds(p, 1), :]
        for c in range(col_blocks):
            for r in range(row_tiles):
                tile = flat[back_slot[(p * row_tiles + r) * col_blocks + c]]
                scaled[p, r * high:(r + 1) * high, c * wide:(c + 1) * wide] = (
                    tile.astype(jnp.float32) * chi[:, c * wide:(c + 1) * wide]).astype(jnp.bfloat16)

    def home_step(g):
        @pl.when((g + 1 >= chunks // 2) & (g + 1 < chunks))
        def _():
            second.relay(g + 1)
        @pl.when(g % PARTS == 0)
        def _():
            unpack(g // PARTS)
        second.arrived(g)
        product(second, g)

    staged(home, back_item_of, home_plan, 0, home_step)
    ahead.sent()
    second.sent_far()
    second.sent_near()
    home.received()

    flat_back = returned.reshape(nboson * capacity, high, wide)
    def finish(q):
        for r in range(row_tiles):
            for c in range(col_blocks):
                tile = flat_back[send_slot[(q * row_tiles + r) * col_blocks + c]]
                at = (q, slice(r * high, (r + 1) * high), slice(c * wide, (c + 1) * wide))
                out[at] = (base[at] + tile.astype(jnp.float32)).astype(jnp.bfloat16)
    loop(0, points, finish)
    home.sent()


def local(nboson, nblock, gamma_ph, full_ph, chi_ph, pp_vertex, chi_pp, relabel):
    points, rows, order = gamma_ph.shape
    row_tiles, col_blocks = relabel.shape[1] // nblock, relabel.shape[2]
    high, wide = rows // row_tiles, order // col_blocks
    total = points * row_tiles * col_blocks
    capacity = -(-total // nboson) + 1
    bf16, f32 = jnp.bfloat16, jnp.float32
    whole = pltpu.VMEM((points, order, order), bf16)
    shard = pltpu.VMEM(gamma_ph.shape, bf16)
    slabs = pltpu.VMEM((nboson, capacity, high, wide), bf16)
    table_rows = -(-(nboson * capacity) // LANES) * 8
    for count in (nboson, points, row_tiles * col_blocks, col_blocks, PARTS):
        assert count & (count - 1) == 0
    vmem = pl.BlockSpec(memory_space=pltpu.VMEM)
    hbm = pl.BlockSpec(memory_space=pl.ANY)
    operands = (relabel.transpose(1, 2, 0), gamma_ph, full_ph, chi_ph, pp_vertex, chi_pp)

    def window(lag):
        result = pltpu.VMEM(gamma_ph.shape, bf16)
        early = lag is not None
        return pl.pallas_call(
            functools.partial(kernel, nboson, nblock, row_tiles, col_blocks, lag),
            out_shape=(result, pltpu.VMEM((8, LANES), jnp.int32)) if early else result,
            name="early" if early else "plain",
            in_specs=[hbm, hbm, hbm, vmem, hbm, vmem], out_specs=(vmem, vmem) if early else vmem,
            scratch_shapes=[
                whole, whole, shard, shard, pltpu.VMEM(gamma_ph.shape, f32),
                pltpu.VMEM((total, high, wide), bf16), slabs, slabs, slabs, slabs,
                pltpu.VMEM(operands[0].shape, jnp.int32),
                pltpu.VMEM((table_rows, LANES), jnp.int32), pltpu.SMEM((table_rows, LANES), jnp.int32),
                DMA, DMA((2,)), DMA((nboson,)), DMA((nboson,)), DMA((nboson,)), DMA((nboson,)),
            ] + gather_scratch(nblock, points) + gather_scratch(nblock, points),
            compiler_params=pltpu.CompilerParams(
                collective_id=int(early), has_side_effects=True, vmem_limit_bytes=60 * 1024 * 1024),
        )(*operands)

    chunks = points * PARTS
    if capacity <= chunks:
        return window(None)
    result, late = window(LAG * chunks // 16)
    return lax.cond(late[0, 0] == 0, lambda: result, lambda: window(None))


LAG = 10


def solution(mesh):
    placed = (
        P("boson", "block", None),
        P("boson", "block", None),
        P("boson", None),
        P("boson", "block", None),
        P("boson", None),
        P(),
    )
    return jax.shard_map(
        functools.partial(local, mesh.shape["boson"], mesh.shape["block"]), mesh=mesh,
        in_specs=placed, out_specs=P("boson", "block", None), check_vma=False,
    )
```

```python
import functools
import jax
import jax.numpy as jnp
from jax import lax
from jax.experimental import pallas as pl
from jax.experimental.pallas import tpu as pltpu
from jax.sharding import PartitionSpec as P

MESH = pl.DeviceIdType.MESH
DMA = pltpu.SemaphoreType.DMA
PARTS = 4
LANES = 128


def loop(start, stop, body):
    lax.fori_loop(start, stop, lambda i, carry: (body(i), carry)[1], 0)


class Schedule:
    def __init__(self, chunks, capacity, start):
        self.chunks, self.capacity, self.start = chunks, capacity, start
        assert 0 < chunks - start < capacity

    def due(self, g):
        return jnp.maximum(g + 1 - self.start, 0)


class Gather:
    def __init__(self, nblock, shard, whole, sems):
        self.nblock, self.shard, self.whole = nblock, shard, whole
        self.far_s, self.far_r, self.near_s, self.near_r, self.fwd_s, self.fwd_r, self.loc = sems
        self.points, self.rows, order = shard.shape
        self.cols = order // PARTS
        self.chunks = self.points * PARTS
        self.boson = lax.axis_index("boson")
        self.here = lax.axis_index("block")
        self.partner = self.here + 1 - 2 * (self.here % 2)

    def peers(self):
        out = [self.partner]
        for j in range(1, self.nblock // 2):
            out.append((self.here + 2 * j) % self.nblock)
        return out

    def columns(self, g):
        return pl.ds(pl.multiple_of(g % PARTS * self.cols, self.cols), self.cols)

    def source(self, g):
        return self.shard.at[g // PARTS, :, self.columns(g)]

    def place(self, g, owner):
        rows = pl.ds(pl.multiple_of(owner * self.rows, self.rows), self.rows)
        return self.whole.at[g // PARTS, rows, self.columns(g)]

    def far(self, g, j, owner):
        return pltpu.make_async_remote_copy(
            src_ref=self.source(g), dst_ref=self.place(g, owner),
            send_sem=self.far_s.at[j - 1, g], recv_sem=self.far_r.at[j - 1, g],
            device_id=(self.boson, (self.here + 2 * j) % self.nblock), device_id_type=MESH)

    def near(self, g, owner):
        return pltpu.make_async_remote_copy(
            src_ref=self.source(g), dst_ref=self.place(g, owner),
            send_sem=self.near_s.at[g], recv_sem=self.near_r.at[g],
            device_id=(self.boson, self.partner), device_id_type=MESH)

    def forward(self, g, j, owner):
        return pltpu.make_async_remote_copy(
            src_ref=self.place(g, owner), dst_ref=self.place(g, owner),
            send_sem=self.fwd_s.at[j - 1, g], recv_sem=self.fwd_r.at[j - 1, g],
            device_id=(self.boson, self.partner), device_id_type=MESH)

    def own(self):
        rows = pl.ds(pl.multiple_of(self.here * self.rows, self.rows), self.rows)
        return pltpu.make_async_copy(self.shard, self.whole.at[:, rows], self.loc)

    def each_far(self, act):
        for j in range(1, self.nblock // 2):
            act(j)

    def start(self):
        def one(g):
            self.each_far(lambda j: self.far(g, j, self.here).start())
            self.near(g, self.here).start()
        loop(0, self.chunks, one)

    def relay(self, g):
        def one(j):
            owner = (self.here + self.nblock - 2 * j) % self.nblock
            self.far(g, j, owner).wait_recv()
            self.forward(g, j, owner).start()
        self.each_far(one)

    def arrived(self, g):
        self.near(g, self.partner).wait_recv()
        def one(j):
            twin = (self.partner + self.nblock - 2 * j) % self.nblock
            self.forward(g, j, twin).wait_recv()
        self.each_far(one)

    def sent_far(self):
        loop(0, self.chunks,
             lambda g: self.each_far(lambda j: self.far(g, j, self.here).wait_send()))

    def sent_near(self):
        def one(g):
            self.near(g, self.here).wait_send()
            def fwd(j):
                owner = (self.here + self.nblock - 2 * j) % self.nblock
                self.forward(g, j, owner).wait_send()
            self.each_far(fwd)
        loop(0, self.chunks, one)


def gather_scratch(nblock, points):
    far, chunks = max(nblock // 2 - 1, 1), points * PARTS
    return [DMA((far, chunks)), DMA((far, chunks)), DMA((chunks,)), DMA((chunks,)),
            DMA((far, chunks)), DMA((far, chunks)), DMA]


class Exchange:
    def __init__(self, nboson, outgoing, incoming, send, recv):
        self.n, self.outgoing, self.incoming = nboson, outgoing, incoming
        self.send, self.recv = send, recv
        self.capacity = outgoing.shape[1]
        self.boson = lax.axis_index("boson")
        self.block = lax.axis_index("block")

    def peers(self):
        return [(self.boson + s) % self.n for s in range(1, self.n)]

    def shift(self, i):
        return self.n // 2 + (1 - 2 * (i % 2)) * ((i + 1) // 2)

    def copy(self, s, slot, start=0, size=None):
        dest = (self.boson + s) % self.n
        slots = pl.ds(start, self.capacity if size is None else size)
        return pltpu.make_async_remote_copy(
            src_ref=self.outgoing.at[dest, slots], dst_ref=self.incoming.at[slot, slots],
            send_sem=self.send.at[s], recv_sem=self.recv.at[s],
            device_id=(dest, self.block), device_id_type=MESH)

    def pack(self, target, dest, tiles, table, start, size):
        for k in range(size):
            target[dest, start + k] = tiles[table[dest * self.capacity + start + k]]

    def part(self, tiles, table, start, size):
        def pack(i):
            dest = (self.boson + self.shift(i)) % self.n
            self.pack(self.outgoing, dest, tiles, table, start, size)
        def send(i):
            self.copy(self.shift(i), self.boson, start, size).start()
        pack(0)
        def one(i):
            pack(i)
            send(i - 1)
        loop(1, self.n - 1, one)
        return lambda: send(self.n - 2)

    def keep(self, tiles, table):
        self.pack(self.incoming, self.boson, tiles, table, 0, self.capacity)

    def received(self):
        loop(1, self.n, lambda s: self.copy(s, (self.boson + self.n - s) % self.n).wait_recv())

    def sent(self):
        loop(1, self.n, lambda s: self.copy(s, self.boson).wait_send())


def greet(block_peers, boson_peers):
    barrier = pltpu.get_barrier_semaphore()
    boson, block = lax.axis_index("boson"), lax.axis_index("block")
    for peer in block_peers:
        pl.semaphore_signal(barrier, inc=1, device_id=(boson, peer), device_id_type=MESH)
    for peer in boson_peers:
        pl.semaphore_signal(barrier, inc=1, device_id=(peer, block), device_id_type=MESH)
    pl.semaphore_wait(barrier, len(block_peers) + len(boson_peers))


def own_targets(nboson, targets, first_row, row_tiles):
    _, col_blocks, count = targets.shape
    points, per_point = count // nboson, row_tiles * col_blocks
    boson = lax.axis_index("boson")
    flat = targets[pl.ds(first_row, row_tiles)].reshape(per_point, count)
    lane = lax.broadcasted_iota(jnp.int32, flat.shape, 1)
    return jnp.concatenate(
        [jnp.sum(jnp.where(lane == boson * points + q, flat, 0), axis=1, keepdims=True)
         for q in range(points)], axis=0)


def decode(nboson, points, col_blocks, per_point, own):
    total = points * per_point
    boson = lax.axis_index("boson")
    item = lax.broadcasted_iota(jnp.int32, (total, 1), 0)
    shift = ((own >> (points.bit_length() - 1)) - boson) & (nboson - 1)
    target = (own & (points - 1)) * per_point + (item & (per_point - 1))
    def chunk(place):
        wide = col_blocks // PARTS
        column = place & (col_blocks - 1)
        return (place >> (per_point.bit_length() - 1)) * PARTS + (column >> (wide.bit_length() - 1))
    return item, shift, target, chunk(item), chunk(target)


def slot_tables(nboson, capacity, targets, row_tiles, rows):
    _, col_blocks, count = targets.shape
    points, per_point = count // nboson, row_tiles * col_blocks
    total = points * per_point
    boson = lax.axis_index("boson")
    own = own_targets(nboson, targets, lax.axis_index("block") * row_tiles, row_tiles)
    item, shift, target, ahead, home = decode(nboson, points, col_blocks, per_point, own)

    def spread(keys, values, width):
        wanted = lax.broadcasted_iota(jnp.int32, (total, width), 1)
        return jnp.sum(jnp.where(keys == wanted, values, 0), axis=0, keepdims=True)

    same = spread(item, shift, total) == shift
    def rank(key):
        later = same & (spread(item, key, total) > key)
        return capacity - 1 - jnp.sum(jnp.where(later, 1, 0), axis=1, keepdims=True)

    there = ((boson + shift) & (nboson - 1)) * capacity
    here = ((boson - shift) & (nboson - 1)) * capacity
    out_rank, back_rank = rank(ahead * total + item), rank(home * total + target)
    width = rows.shape[0] // 8 * rows.shape[1]
    last_slot, last_item = nboson * capacity - 1, total - 1
    for k, (keys, values, last) in enumerate((
            (item, there + back_rank, last_slot), (there + out_rank, item, last_item),
            (target, here + out_rank, last_slot), (here + back_rank, target, last_item))):
        line = jnp.clip(spread(keys, values, width), 0, last)
        for h in range(width // LANES):
            rows[h * 8 + k:h * 8 + k + 1, :] = line[:, h * LANES:(h + 1) * LANES]


def late_tiles(nboson, targets, row_tiles, schedules):
    row_count, col_blocks, count = targets.shape
    points, per_point = count // nboson, row_tiles * col_blocks
    total, chunks = points * per_point, points * PARTS
    lane = lax.broadcasted_iota(jnp.int32, (total, chunks * nboson), 1)
    wanted, upto = lane & (nboson - 1), lane >> (nboson.bit_length() - 1)
    late = 0
    for b in range(row_count // row_tiles):
        own = own_targets(nboson, targets, b * row_tiles, row_tiles)
        _, shift, _, *arrivals = decode(nboson, points, col_blocks, per_point, own)
        match = shift == wanted
        number = jnp.sum(jnp.where(match, 1, 0), axis=0, keepdims=True)
        for arrival, schedule in zip(arrivals, schedules):
            ready = jnp.sum(jnp.where(match & (arrival <= upto), 1, 0), axis=0, keepdims=True)
            due = schedule.due(upto[0:1]) - (schedule.capacity - number)
            late = late + jnp.where((ready < due) & (wanted[0:1] > 0), 1, 0)
    return jnp.sum(late, axis=1, keepdims=True)


class Table:
    def __init__(self, ref, k):
        self.ref, self.k = ref, k

    def __getitem__(self, i):
        return self.ref[i // LANES * 8 + self.k, i % LANES]


def kernel(nboson, nblock, row_tiles, col_blocks, lag, *refs):
    relabel, gamma_in, full_in, chi_ph, pp_in, chi_pp, out, *refs = refs
    late, refs = (refs[0], refs[1:]) if lag is not None else (None, refs)
    (full, pp, gamma, scaled, base, tiles, packed, landed, back, returned,
     targets, table_rows, table,
     gamma_sem, table_sem, ahead_s, ahead_r, home_s, home_r, *gather_sems) = refs
    half = len(gather_sems) // 2
    first = Gather(nblock, full_in, full, gather_sems[:half])
    second = Gather(nblock, pp_in, pp, gather_sems[half:])
    ahead = Exchange(nboson, packed, landed, ahead_s, ahead_r)
    home = Exchange(nboson, back, returned, home_s, home_r)
    points, rows, order = gamma.shape
    chunks = first.chunks
    high, wide = rows // row_tiles, order // col_blocks
    capacity = landed.shape[1]
    send_slot, item_of, back_slot, back_item_of = (Table(table, i) for i in range(4))
    load_targets = pltpu.make_async_copy(relabel, targets, table_sem.at[0])
    load_table = pltpu.make_async_copy(table_rows, table, table_sem.at[1])
    load_gamma = pltpu.make_async_copy(gamma_in, gamma, gamma_sem)

    first.own().start()
    load_gamma.start()
    load_targets.start()
    second.own().start()
    greet(first.peers(), ahead.peers())
    first.start()

    load_gamma.wait()
    for q in range(points):
        scaled[q] = (gamma[q].astype(jnp.float32) * chi_ph[q:q + 1, :]).astype(jnp.bfloat16)
    load_targets.wait()
    slot_tables(nboson, capacity, targets, row_tiles, table_rows)
    load_table.start()
    if lag is None:
        ahead_plan = home_plan = None
    else:
        ahead_plan = Schedule(chunks, capacity, lag)
        home_plan = Schedule(chunks, capacity, lag)
        late[...] = jnp.broadcast_to(
            late_tiles(nboson, targets, row_tiles, (ahead_plan, home_plan)), late.shape)
    first.own().wait()
    load_table.wait()

    def cut(wire, g):
        q, column = g // PARTS, g % PARTS * (first.cols // wide)
        for r in range(row_tiles):
            for k in range(first.cols // wide):
                item = (q * row_tiles + r) * col_blocks + column + k
                tiles[item] = wire[r * high:(r + 1) * high, k * wide:(k + 1) * wide]

    def product(gather, g):
        q, at = g // PARTS, gather.columns(g)
        phi = jnp.dot(scaled[q], gather.whole[q, :, at], preferred_element_type=jnp.float32)
        cut(phi.astype(jnp.bfloat16), g)
        return q, at, phi

    def ph(g):
        first.arrived(g)
        q, at, phi = product(first, g)
        base[q, :, at] = gamma[q, :, at].astype(jnp.float32) + phi

    def staged(exchange, table, plan, begin, step):
        if plan is None:
            loop(begin, chunks, step)
            sent = 0
        else:
            loop(begin, plan.start, step)
            def one(g):
                step(g)
                exchange.part(tiles, table, g - plan.start, 1)()
            loop(plan.start, chunks, one)
            sent = chunks - plan.start
        last = exchange.part(tiles, table, sent, capacity - sent)
        exchange.keep(tiles, table)
        last()

    def ahead_step(g):
        @pl.when(g + 1 < chunks)
        def _():
            first.relay(g + 1)
        @pl.when(g == chunks - 2)
        def _():
            second.start()
        ph(g)

    first.relay(0)
    staged(ahead, item_of, ahead_plan, 0, ahead_step)
    first.sent_far()
    first.sent_near()
    second.own().wait()
    loop(0, chunks // 2, second.relay)
    ahead.received()

    flat = landed.reshape(nboson * capacity, high, wide)
    def unpack(p):
        chi = chi_pp[pl.ds(p, 1), :]
        for c in range(col_blocks):
            for r in range(row_tiles):
                tile = flat[back_slot[(p * row_tiles + r) * col_blocks + c]]
                scaled[p, r * high:(r + 1) * high, c * wide:(c + 1) * wide] = (
                    tile.astype(jnp.float32) * chi[:, c * wide:(c + 1) * wide]).astype(jnp.bfloat16)

    def home_step(g):
        @pl.when((g + 1 >= chunks // 2) & (g + 1 < chunks))
        def _():
            second.relay(g + 1)
        @pl.when(g % PARTS == 0)
        def _():
            unpack(g // PARTS)
        second.arrived(g)
        product(second, g)

    staged(home, back_item_of, home_plan, 0, home_step)
    ahead.sent()
    second.sent_far()
    second.sent_near()
    home.received()

    flat_back = returned.reshape(nboson * capacity, high, wide)
    def finish(q):
        for r in range(row_tiles):
            for c in range(col_blocks):
                tile = flat_back[send_slot[(q * row_tiles + r) * col_blocks + c]]
                at = (q, slice(r * high, (r + 1) * high), slice(c * wide, (c + 1) * wide))
                out[at] = (base[at] + tile.astype(jnp.float32)).astype(jnp.bfloat16)
    loop(0, points, finish)
    home.sent()


def local(nboson, nblock, gamma_ph, full_ph, chi_ph, pp_vertex, chi_pp, relabel):
    points, rows, order = gamma_ph.shape
    row_tiles, col_blocks = relabel.shape[1] // nblock, relabel.shape[2]
    high, wide = rows // row_tiles, order // col_blocks
    total = points * row_tiles * col_blocks
    capacity = -(-total // nboson) + 1
    bf16, f32 = jnp.bfloat16, jnp.float32
    whole = pltpu.VMEM((points, order, order), bf16)
    shard = pltpu.VMEM(gamma_ph.shape, bf16)
    slabs = pltpu.VMEM((nboson, capacity, high, wide), bf16)
    table_rows = -(-(nboson * capacity) // LANES) * 8
    for count in (nboson, points, row_tiles * col_blocks, col_blocks, PARTS):
        assert count & (count - 1) == 0
    vmem = pl.BlockSpec(memory_space=pltpu.VMEM)
    hbm = pl.BlockSpec(memory_space=pl.ANY)
    operands = (relabel.transpose(1, 2, 0), gamma_ph, full_ph, chi_ph, pp_vertex, chi_pp)

    def window(lag):
        result = pltpu.VMEM(gamma_ph.shape, bf16)
        early = lag is not None
        return pl.pallas_call(
            functools.partial(kernel, nboson, nblock, row_tiles, col_blocks, lag),
            out_shape=(result, pltpu.VMEM((8, LANES), jnp.int32)) if early else result,
            name="early" if early else "plain",
            in_specs=[hbm, hbm, hbm, vmem, hbm, vmem], out_specs=(vmem, vmem) if early else vmem,
            scratch_shapes=[
                whole, whole, shard, shard, pltpu.VMEM(gamma_ph.shape, f32),
                pltpu.VMEM((total, high, wide), bf16), slabs, slabs, slabs, slabs,
                pltpu.VMEM(operands[0].shape, jnp.int32),
                pltpu.VMEM((table_rows, LANES), jnp.int32), pltpu.SMEM((table_rows, LANES), jnp.int32),
                DMA, DMA((2,)), DMA((nboson,)), DMA((nboson,)), DMA((nboson,)), DMA((nboson,)),
            ] + gather_scratch(nblock, points) + gather_scratch(nblock, points),
            compiler_params=pltpu.CompilerParams(
                collective_id=int(early), has_side_effects=True, vmem_limit_bytes=60 * 1024 * 1024),
        )(*operands)

    chunks = points * PARTS
    if capacity <= chunks:
        return window(None)
    result, late = window(LAG * chunks // 16)
    return lax.cond(late[0, 0] == 0, lambda: result, lambda: window(None))


LAG = 6


def solution(mesh):
    placed = (
        P("boson", "block", None),
        P("boson", "block", None),
        P("boson", None),
        P("boson", "block", None),
        P("boson", None),
        P(),
    )
    return jax.shard_map(
        functools.partial(local, mesh.shape["boson"], mesh.shape["block"]), mesh=mesh,
        in_specs=placed, out_specs=P("boson", "block", None), check_vma=False,
    )
```

```python
import functools
import jax
import jax.numpy as jnp
from jax import lax
from jax.experimental import pallas as pl
from jax.experimental.pallas import tpu as pltpu
from jax.sharding import PartitionSpec as P

MESH = pl.DeviceIdType.MESH
DMA = pltpu.SemaphoreType.DMA
PARTS = 4
FIXED = 2
LAG = 3
LANES = 128


def loop(start, stop, body):
    lax.fori_loop(start, stop, lambda i, carry: (body(i), carry)[1], 0)


class Gather:
    def __init__(self, nblock, shard, blocks, whole, fixed, sems):
        self.nblock, self.shard, self.blocks, self.whole = nblock, shard, blocks, whole
        self.far_s, self.far_r, self.near_s, self.near_r, self.fwd_s, self.fwd_r, self.loc = sems
        self.chunks, _, self.cols = whole.shape
        self.rows = shard.shape[1]
        self.fixed = fixed
        self.boson = lax.axis_index("boson")
        self.here = lax.axis_index("block")
        self.partner = self.here + 1 - 2 * (self.here % 2)

    def peers(self):
        out = [self.partner]
        for j in range(1, self.nblock // 2):
            out.append((self.here + 2 * j) % self.nblock)
        return out

    def place(self, g, owner):
        rows = pl.ds(pl.multiple_of(owner * self.rows, self.rows), self.rows)
        return self.whole.at[g, rows]

    def load(self, g):
        source = self.shard.at[g // PARTS, :, g % PARTS * self.cols:(g % PARTS + 1) * self.cols]
        target = self.place(g, self.here) if g < self.fixed else self.blocks.at[g]
        return pltpu.make_async_copy(source, target, self.loc.at[g])

    def pack(self, order):
        def one(g):
            self.place(g, self.here)[...] = self.blocks[order(g)]
        loop(self.fixed, self.chunks, one)

    def far(self, g, j, owner):
        return pltpu.make_async_remote_copy(
            src_ref=self.place(g, owner), dst_ref=self.place(g, owner),
            send_sem=self.far_s.at[j - 1, g], recv_sem=self.far_r.at[j - 1, g],
            device_id=(self.boson, (self.here + 2 * j) % self.nblock), device_id_type=MESH)

    def near(self, g, owner):
        return pltpu.make_async_remote_copy(
            src_ref=self.place(g, owner), dst_ref=self.place(g, owner),
            send_sem=self.near_s.at[g], recv_sem=self.near_r.at[g],
            device_id=(self.boson, self.partner), device_id_type=MESH)

    def forward(self, g, j, owner):
        return pltpu.make_async_remote_copy(
            src_ref=self.place(g, owner), dst_ref=self.place(g, owner),
            send_sem=self.fwd_s.at[j - 1, g], recv_sem=self.fwd_r.at[j - 1, g],
            device_id=(self.boson, self.partner), device_id_type=MESH)

    def each_far(self, act):
        for j in range(1, self.nblock // 2):
            act(j)

    def start(self, begin, end):
        def one(g):
            self.each_far(lambda j: self.far(g, j, self.here).start())
            self.near(g, self.here).start()
        loop(begin, end, one)

    def relay(self, g):
        def one(j):
            owner = (self.here + self.nblock - 2 * j) % self.nblock
            self.far(g, j, owner).wait_recv()
            self.forward(g, j, owner).start()
        self.each_far(one)

    def arrived(self, g):
        self.near(g, self.partner).wait_recv()
        def one(j):
            twin = (self.partner + self.nblock - 2 * j) % self.nblock
            self.forward(g, j, twin).wait_recv()
        self.each_far(one)

    def sent(self):
        def one(g):
            self.each_far(lambda j: self.far(g, j, self.here).wait_send())
            self.near(g, self.here).wait_send()
            def fwd(j):
                owner = (self.here + self.nblock - 2 * j) % self.nblock
                self.forward(g, j, owner).wait_send()
            self.each_far(fwd)
        loop(0, self.chunks, one)


def gather_scratch(nblock, points):
    far, chunks = max(nblock // 2 - 1, 1), points * PARTS
    return [DMA((far, chunks)), DMA((far, chunks)), DMA((chunks,)), DMA((chunks,)),
            DMA((far, chunks)), DMA((far, chunks)), DMA((chunks,))]


class Exchange:
    def __init__(self, nboson, outgoing, incoming, send, recv):
        self.n, self.outgoing, self.incoming = nboson, outgoing, incoming
        self.send, self.recv = send, recv
        self.capacity = outgoing.shape[1]
        self.boson = lax.axis_index("boson")
        self.block = lax.axis_index("block")

    def peers(self):
        return [(self.boson + s) % self.n for s in range(1, self.n)]

    def shift(self, i):
        return self.n // 2 + (1 - 2 * (i % 2)) * ((i + 1) // 2)

    def copy(self, s, slot, start=0, size=None):
        dest = (self.boson + s) % self.n
        slots = pl.ds(start, self.capacity if size is None else size)
        return pltpu.make_async_remote_copy(
            src_ref=self.outgoing.at[dest, slots], dst_ref=self.incoming.at[slot, slots],
            send_sem=self.send.at[s], recv_sem=self.recv.at[s],
            device_id=(dest, self.block), device_id_type=MESH)

    def pack(self, target, dest, tiles, table, start, size):
        for k in range(size):
            target[dest, start + k] = tiles[table[dest * self.capacity + start + k]]

    def part(self, tiles, table, start, size):
        def pack(i):
            dest = (self.boson + self.shift(i)) % self.n
            self.pack(self.outgoing, dest, tiles, table, start, size)
        def send(i):
            self.copy(self.shift(i), self.boson, start, size).start()
        pack(0)
        def one(i):
            pack(i)
            send(i - 1)
        loop(1, self.n - 1, one)
        return lambda: send(self.n - 2)

    def keep(self, tiles, table):
        self.pack(self.incoming, self.boson, tiles, table, 0, self.capacity)

    def received(self):
        loop(1, self.n, lambda s: self.copy(s, (self.boson + self.n - s) % self.n).wait_recv())

    def sent(self):
        loop(1, self.n, lambda s: self.copy(s, self.boson).wait_send())


def greet(block_peers, boson_peers):
    barrier = pltpu.get_barrier_semaphore()
    boson, block = lax.axis_index("boson"), lax.axis_index("block")
    for peer in block_peers:
        pl.semaphore_signal(barrier, inc=1, device_id=(boson, peer), device_id_type=MESH)
    for peer in boson_peers:
        pl.semaphore_signal(barrier, inc=1, device_id=(peer, block), device_id_type=MESH)
    pl.semaphore_wait(barrier, len(block_peers) + len(boson_peers))


def bits(count):
    return count.bit_length() - 1


class Items:
    def __init__(self, nboson, targets, first_row, row_tiles):
        _, col_blocks, count = targets.shape
        points, per_point = count // nboson, row_tiles * col_blocks
        self.total, self.chunks, self.pair = points * per_point, points * PARTS, col_blocks // PARTS
        self.row_tiles = row_tiles
        boson = lax.axis_index("boson")
        flat = targets[pl.ds(first_row, row_tiles)].reshape(per_point, count)
        lane = lax.broadcasted_iota(jnp.int32, flat.shape, 1)
        own = jnp.concatenate(
            [jnp.sum(jnp.where(lane == boson * points + q, flat, 0), axis=1, keepdims=True)
             for q in range(points)], axis=0)
        self.item = lax.broadcasted_iota(jnp.int32, (self.total, 1), 0)
        self.shift = ((own >> bits(points)) - boson) & (nboson - 1)
        self.row = (self.item >> bits(col_blocks)) & (row_tiles - 1)
        self.column = self.item & (col_blocks - 1)
        self.target = (own & (points - 1)) * per_point + (self.item & (per_point - 1))
        part = self.column >> bits(self.pair)
        self.ahead = (self.item >> bits(per_point)) * PARTS + part
        self.home = (own & (points - 1)) * PARTS + part

    def spread(self, keys, values, width):
        wanted = lax.broadcasted_iota(jnp.int32, (self.total, width), 1)
        return jnp.sum(jnp.where(keys == wanted, values, 0), axis=0, keepdims=True)

    def tile(self, chunk, places):
        if places is not None:
            lane = lax.broadcasted_iota(jnp.int32, (self.total, places.shape[1]), 1)
            chunk = jnp.sum(jnp.where(chunk == lane, places, 0), axis=1, keepdims=True)
        return (chunk * self.row_tiles + self.row) * self.pair + (self.column & (self.pair - 1))


def slot_tables(nboson, capacity, items, ahead_places, home_places, rows):
    boson = lax.axis_index("boson")
    same = items.spread(items.item, items.shift, items.total) == items.shift
    def rank(key):
        later = same & (items.spread(items.item, key, items.total) > key)
        return capacity - 1 - jnp.sum(jnp.where(later, 1, 0), axis=1, keepdims=True)

    there = ((boson + items.shift) & (nboson - 1)) * capacity
    here = ((boson - items.shift) & (nboson - 1)) * capacity
    ahead = items.tile(items.ahead, ahead_places)
    home = items.tile(items.home, home_places)
    out_rank, back_rank = rank(ahead), rank(home)
    width = rows.shape[0] // 8 * rows.shape[1]
    last_slot, last_item = nboson * capacity - 1, items.total - 1
    for k, (keys, values, last) in enumerate((
            (items.item, there + back_rank, last_slot), (there + out_rank, ahead, last_item),
            (items.target, here + out_rank, last_slot), (here + back_rank, home, last_item))):
        line = jnp.clip(items.spread(keys, values, width), 0, last)
        for h in range(width // LANES):
            rows[h * 8 + k:h * 8 + k + 1, :] = line[:, h * LANES:(h + 1) * LANES]


def choose_orders(nboson, nblock, capacity, fixed, lag, targets, row_tiles, rows):
    def counts(pick, items_of):
        total = 0.
        for b, items in enumerate(items_of):
            lane = lax.broadcasted_iota(jnp.int32, (items.total, LANES), 1)
            hot = jnp.where(lane == b * nboson + items.shift, 1., 0.).astype(jnp.bfloat16)
            chunk = items.spread(items.item, pick(items), items.total)
            turn = lax.broadcasted_iota(jnp.int32, (items.chunks, items.total), 0)
            member = jnp.where(chunk == turn, 1., 0.).astype(jnp.bfloat16)
            total = total + jnp.dot(member, hot, preferred_element_type=jnp.float32)
        return total

    items_of = [Items(nboson, targets, b * row_tiles, row_tiles) for b in range(nblock)]
    chunks = items_of[0].chunks
    lane = lax.broadcasted_iota(jnp.int32, (1, LANES), 1)
    weighed = (lane < nboson * nblock) & ((lane & (nboson - 1)) > 0)
    chunk = lax.broadcasted_iota(jnp.int32, (chunks, 1), 0)
    tables, begin = [], []
    for pick in (lambda i: i.ahead, lambda i: i.home):
        count = counts(pick, items_of)
        gain = jnp.exp(-jnp.minimum(count, 60.))
        spare = capacity - jnp.sum(count, axis=0, keepdims=True)
        held = jnp.sum(jnp.where(chunk < fixed, count, 0.), axis=0, keepdims=True)
        tables.append((count, gain, spare))
        begin.append((jnp.where(weighed, jnp.exp(jnp.clip(-spare - held, -60., 60.)), 0.),
                      jnp.broadcast_to(jnp.where(chunk < fixed, chunk, -1), (chunks, LANES))))

    def choose(t, state):
        out = []
        for (weight, turn), (_, gain, _) in zip(state, tables):
            score = jnp.sum(weight * gain, axis=1, keepdims=True)
            score = jnp.where(turn < 0, score, jnp.inf)
            best = jnp.min(score, axis=0, keepdims=True)
            index = lax.broadcasted_iota(jnp.int32, score.shape, 0)
            hit = index == jnp.min(jnp.where(score == best, index, chunks), axis=0, keepdims=True)
            weight = weight * jnp.sum(jnp.where(hit, gain, 0.), axis=0, keepdims=True)
            out.append((weight, jnp.where(hit, t, turn)))
        return tuple(out)

    chosen = lax.fori_loop(fixed, chunks, choose, tuple(begin))
    late = jnp.zeros((1, LANES), jnp.float32)
    turns = []
    for k, ((_, turn), (count, _, spare)) in enumerate(zip(chosen, tables)):
        index = lax.broadcasted_iota(jnp.int32, turn.shape, 0)
        column = lax.broadcasted_iota(jnp.int32, turn.shape, 1)
        order = jnp.sum(jnp.where(turn == column, index, 0), axis=0, keepdims=True)
        rows[k:k + 1, :] = jnp.clip(order, 0, chunks - 1)
        turned = jnp.sum(jnp.where(index == column, turn, 0), axis=0, keepdims=True)
        turns.append(jnp.clip(turned, 0, chunks - 1))
        rows[k + 2:k + 3, :] = turns[k]
        for g in range(lag, chunks):
            ready = jnp.sum(jnp.where(turn <= g, count, 0.), axis=0, keepdims=True)
            late = late + jnp.where(weighed & (ready + spare < g + 1 - lag), 1., 0.)
    return turns, jnp.sum(late, axis=1, keepdims=True)


class Table:
    def __init__(self, ref, k):
        self.ref, self.k = ref, k

    def __getitem__(self, i):
        return self.ref[i // LANES * 8 + self.k, i % LANES]


def kernel(nboson, nblock, row_tiles, col_blocks, lag, *refs):
    relabel, gamma_in, full_in, chi_ph, pp_in, chi_pp, out, *refs = refs
    early = lag is not None
    late, refs = (refs[0], refs[1:]) if early else (None, refs)
    (full, pp, full_blocks, pp_blocks, gamma, scaled, base, tiles, packed, landed, back, returned,
     targets, table_rows, table, order_rows, orders,
     gamma_sem, table_sem, ahead_s, ahead_r, home_s, home_r, *gather_sems) = refs
    half = len(gather_sems) // 2
    chunks = full.shape[0]
    fixed = FIXED if early else chunks
    first = Gather(nblock, full_in, full_blocks, full, fixed, gather_sems[:half])
    second = Gather(nblock, pp_in, pp_blocks, pp, fixed, gather_sems[half:])
    ahead = Exchange(nboson, packed, landed, ahead_s, ahead_r)
    home = Exchange(nboson, back, returned, home_s, home_r)
    points, rows, order = gamma.shape
    high, wide = rows // row_tiles, order // col_blocks
    pair = first.cols // wide
    capacity = landed.shape[1]
    send_slot, item_of, back_slot, back_item_of = (Table(table, i) for i in range(4))
    load_targets = pltpu.make_async_copy(relabel, targets, table_sem.at[0])
    load_table = pltpu.make_async_copy(table_rows, table, table_sem.at[1])
    load_gamma = pltpu.make_async_copy(gamma_in, gamma, gamma_sem)

    load_targets.start()
    for g in range(chunks):
        first.load(g).start()
    load_gamma.start()
    for g in range(chunks):
        second.load(g).start()
    greet(first.peers(), ahead.peers())
    for g in range(fixed):
        first.load(g).wait()
    first.start(0, fixed)

    load_targets.wait()
    if early:
        turns, count = choose_orders(
            nboson, nblock, capacity, fixed, lag, targets, row_tiles, order_rows)
        load_orders = pltpu.make_async_copy(order_rows, orders, table_sem.at[2])
        load_orders.start()
        late[...] = jnp.broadcast_to(count, late.shape)
        for g in range(fixed, chunks):
            first.load(g).wait()
        load_orders.wait()
        first.pack(lambda g: orders[0, g])
    else:
        turns = None, None

    items = Items(nboson, targets, lax.axis_index("block") * row_tiles, row_tiles)
    slot_tables(nboson, capacity, items, *turns, table_rows)
    if early:
        first.start(fixed, chunks)
    load_table.start()
    load_gamma.wait()
    for q in range(points):
        scaled[q] = (gamma[q].astype(jnp.float32) * chi_ph[q:q + 1, :]).astype(jnp.bfloat16)
    load_table.wait()

    def product(gather, g, k):
        point = (orders[k, g] if early else g) // PARTS
        phi = jnp.dot(scaled[point], gather.whole[g], preferred_element_type=jnp.float32)
        wire = phi.astype(jnp.bfloat16)
        for r in range(row_tiles):
            for i in range(pair):
                tiles[(g * row_tiles + r) * pair + i] = (
                    wire[r * high:(r + 1) * high, i * wide:(i + 1) * wide])
        return phi

    def staged(exchange, table, step):
        begin = lag if early else chunks
        loop(0, begin, step)
        def one(g):
            step(g)
            exchange.part(tiles, table, g - begin, 1)()
        loop(begin, chunks, one)
        last = exchange.part(tiles, table, chunks - begin, capacity - (chunks - begin))
        exchange.keep(tiles, table)
        last()

    def ahead_step(g):
        first.relay(g)
        @pl.when(g == chunks - 2)
        def _():
            for i in range(chunks):
                second.load(i).wait()
            if early:
                second.pack(lambda i: orders[1, i])
        @pl.when(g == chunks - 1)
        def _():
            second.start(0, chunks)
        first.arrived(g)
        base[g] = product(first, g, 0)

    staged(ahead, item_of, ahead_step)
    first.sent()
    waiting = chunks // 4
    loop(0, waiting, second.relay)
    ahead.received()

    flat = landed.reshape(nboson * capacity, high, wide)
    def unpack(p):
        chi = chi_pp[pl.ds(p, 1), :]
        for c in range(col_blocks):
            for r in range(row_tiles):
                tile = flat[back_slot[(p * row_tiles + r) * col_blocks + c]]
                scaled[p, r * high:(r + 1) * high, c * wide:(c + 1) * wide] = (
                    tile.astype(jnp.float32) * chi[:, c * wide:(c + 1) * wide]).astype(jnp.bfloat16)
    loop(0, points, unpack)

    def home_step(g):
        @pl.when(g >= waiting)
        def _():
            second.relay(g)
        second.arrived(g)
        product(second, g, 1)

    staged(home, back_item_of, home_step)
    ahead.sent()
    second.sent()
    home.received()

    flat_back = returned.reshape(nboson * capacity, high, wide)
    def finish(q):
        for c in range(col_blocks):
            chunk = q * PARTS + c // pair
            turn = orders[2, chunk] if early else chunk
            for r in range(row_tiles):
                tile = flat_back[send_slot[(q * row_tiles + r) * col_blocks + c]]
                at = (q, slice(r * high, (r + 1) * high), slice(c * wide, (c + 1) * wide))
                phi = base[turn, r * high:(r + 1) * high, c % pair * wide:(c % pair + 1) * wide]
                total = gamma[at].astype(jnp.float32) + phi + tile.astype(jnp.float32)
                out[at] = total.astype(jnp.bfloat16)
    loop(0, points, finish)
    home.sent()


def local(nboson, nblock, gamma_ph, full_ph, chi_ph, pp_vertex, chi_pp, relabel):
    points, rows, order = gamma_ph.shape
    row_tiles, col_blocks = relabel.shape[1] // nblock, relabel.shape[2]
    high, wide = rows // row_tiles, order // col_blocks
    total = points * row_tiles * col_blocks
    capacity = -(-total // nboson) + 1
    bf16, f32 = jnp.bfloat16, jnp.float32
    chunks, cols = points * PARTS, order // PARTS
    whole = pltpu.VMEM((chunks, order, cols), bf16)
    blocks = pltpu.VMEM((chunks, rows, cols), bf16)
    shard = pltpu.VMEM(gamma_ph.shape, bf16)
    slabs = pltpu.VMEM((nboson, capacity, high, wide), bf16)
    table_rows = -(-(nboson * capacity) // LANES) * 8
    for count in (nboson, points, row_tiles * col_blocks, col_blocks, PARTS):
        assert count & (count - 1) == 0
    vmem = pl.BlockSpec(memory_space=pltpu.VMEM)
    hbm = pl.BlockSpec(memory_space=pl.ANY)
    operands = (relabel.transpose(1, 2, 0), gamma_ph, full_ph, chi_ph, pp_vertex, chi_pp)

    def window(lag):
        result = pltpu.VMEM(gamma_ph.shape, bf16)
        early = lag is not None
        return pl.pallas_call(
            functools.partial(kernel, nboson, nblock, row_tiles, col_blocks, lag),
            out_shape=(result, pltpu.VMEM((8, LANES), jnp.float32)) if early else result,
            name="early" if early else "plain",
            in_specs=[hbm, hbm, hbm, vmem, hbm, vmem], out_specs=(vmem, vmem) if early else vmem,
            scratch_shapes=[
                whole, whole, blocks, blocks, shard, shard, pltpu.VMEM((chunks, rows, cols), f32),
                pltpu.VMEM((total, high, wide), bf16), slabs, slabs, slabs, slabs,
                pltpu.VMEM(operands[0].shape, jnp.int32),
                pltpu.VMEM((table_rows, LANES), jnp.int32), pltpu.SMEM((table_rows, LANES), jnp.int32),
                pltpu.VMEM((8, LANES), jnp.int32), pltpu.SMEM((8, LANES), jnp.int32),
                DMA, DMA((3,)), DMA((nboson,)), DMA((nboson,)), DMA((nboson,)), DMA((nboson,)),
            ] + gather_scratch(nblock, points) + gather_scratch(nblock, points),
            compiler_params=pltpu.CompilerParams(
                collective_id=int(early), has_side_effects=True, vmem_limit_bytes=60 * 1024 * 1024),
        )(*operands)

    if capacity <= chunks - LAG or nboson * nblock > LANES:
        return window(None)
    result, late = window(LAG)
    return lax.cond(late[0, 0] == 0, lambda: result, lambda: window(None))


def solution(mesh):
    placed = (
        P("boson", "block", None),
        P("boson", "block", None),
        P("boson", None),
        P("boson", "block", None),
        P("boson", None),
        P(),
    )
    return jax.shard_map(
        functools.partial(local, mesh.shape["boson"], mesh.shape["block"]), mesh=mesh,
        in_specs=placed, out_specs=P("boson", "block", None), check_vma=False,
    )
```

```python
import functools
import jax
import jax.numpy as jnp
from jax import lax
from jax.experimental import pallas as pl
from jax.experimental.pallas import tpu as pltpu
from jax.sharding import PartitionSpec as P

MESH = pl.DeviceIdType.MESH
DMA = pltpu.SemaphoreType.DMA
PARTS = 4
FIXED = 2
LAG = 2
LANES = 128


def loop(start, stop, body):
    lax.fori_loop(start, stop, lambda i, carry: (body(i), carry)[1], 0)


class Gather:
    def __init__(self, nblock, shard, blocks, whole, fixed, sems):
        self.nblock, self.shard, self.blocks, self.whole = nblock, shard, blocks, whole
        self.far_s, self.far_r, self.near_s, self.near_r, self.fwd_s, self.fwd_r, self.loc = sems
        self.chunks, _, self.cols = whole.shape
        self.rows = shard.shape[1]
        self.fixed = fixed
        self.boson = lax.axis_index("boson")
        self.here = lax.axis_index("block")
        self.partner = self.here + 1 - 2 * (self.here % 2)

    def peers(self):
        out = [self.partner]
        for j in range(1, self.nblock // 2):
            out.append((self.here + 2 * j) % self.nblock)
        return out

    def place(self, g, owner):
        rows = pl.ds(pl.multiple_of(owner * self.rows, self.rows), self.rows)
        return self.whole.at[g, rows]

    def load(self, g):
        source = self.shard.at[g // PARTS, :, g % PARTS * self.cols:(g % PARTS + 1) * self.cols]
        target = self.place(g, self.here) if g < self.fixed else self.blocks.at[g]
        return pltpu.make_async_copy(source, target, self.loc.at[g])

    def pack(self, order):
        def one(g):
            self.place(g, self.here)[...] = self.blocks[order(g)]
        loop(self.fixed, self.chunks, one)

    def far(self, g, j, owner):
        return pltpu.make_async_remote_copy(
            src_ref=self.place(g, owner), dst_ref=self.place(g, owner),
            send_sem=self.far_s.at[j - 1, g], recv_sem=self.far_r.at[j - 1, g],
            device_id=(self.boson, (self.here + 2 * j) % self.nblock), device_id_type=MESH)

    def near(self, g, owner):
        return pltpu.make_async_remote_copy(
            src_ref=self.place(g, owner), dst_ref=self.place(g, owner),
            send_sem=self.near_s.at[g], recv_sem=self.near_r.at[g],
            device_id=(self.boson, self.partner), device_id_type=MESH)

    def forward(self, g, j, owner):
        return pltpu.make_async_remote_copy(
            src_ref=self.place(g, owner), dst_ref=self.place(g, owner),
            send_sem=self.fwd_s.at[j - 1, g], recv_sem=self.fwd_r.at[j - 1, g],
            device_id=(self.boson, self.partner), device_id_type=MESH)

    def each_far(self, act):
        for j in range(1, self.nblock // 2):
            act(j)

    def start_far(self, begin, end):
        loop(begin, end, lambda g: self.each_far(lambda j: self.far(g, j, self.here).start()))

    def start_near(self, begin, end):
        loop(begin, end, lambda g: self.near(g, self.here).start())

    def relay(self, g):
        def one(j):
            owner = (self.here + self.nblock - 2 * j) % self.nblock
            self.far(g, j, owner).wait_recv()
            self.forward(g, j, owner).start()
        self.each_far(one)

    def arrived(self, g):
        self.near(g, self.partner).wait_recv()
        def one(j):
            twin = (self.partner + self.nblock - 2 * j) % self.nblock
            self.forward(g, j, twin).wait_recv()
        self.each_far(one)

    def left(self, g):
        self.each_far(lambda j: self.far(g, j, self.here).wait_send())

    def sent(self, begin, end):
        loop(begin, end, self.left)
        def one(g):
            self.near(g, self.here).wait_send()
            def fwd(j):
                owner = (self.here + self.nblock - 2 * j) % self.nblock
                self.forward(g, j, owner).wait_send()
            self.each_far(fwd)
        loop(0, self.chunks, one)


def gather_scratch(nblock, points):
    far, chunks = max(nblock // 2 - 1, 1), points * PARTS
    return [DMA((far, chunks)), DMA((far, chunks)), DMA((chunks,)), DMA((chunks,)),
            DMA((far, chunks)), DMA((far, chunks)), DMA((chunks,))]


class Exchange:
    def __init__(self, nboson, outgoing, incoming, send, recv):
        self.n, self.outgoing, self.incoming = nboson, outgoing, incoming
        self.send, self.recv = send, recv
        self.capacity = outgoing.shape[1]
        self.boson = lax.axis_index("boson")
        self.block = lax.axis_index("block")

    def peers(self):
        return [(self.boson + s) % self.n for s in range(1, self.n)]

    def shift(self, i):
        return self.n // 2 + (1 - 2 * (i % 2)) * ((i + 1) // 2)

    def copy(self, s, slot, start=0, size=None):
        dest = (self.boson + s) % self.n
        slots = pl.ds(start, self.capacity if size is None else size)
        return pltpu.make_async_remote_copy(
            src_ref=self.outgoing.at[dest, slots], dst_ref=self.incoming.at[slot, slots],
            send_sem=self.send.at[s], recv_sem=self.recv.at[s],
            device_id=(dest, self.block), device_id_type=MESH)

    def pack(self, target, dest, tiles, table, start, size):
        for k in range(size):
            target[dest, start + k] = tiles[table[dest * self.capacity + start + k]]

    def part(self, tiles, table, start, size, first=False, last=False):
        behind = (start if first else start - 1, size - first + last)
        def pack(i, slots):
            dest = (self.boson + self.shift(i)) % self.n
            self.pack(self.outgoing, dest, tiles, table, *slots)
        def send(i, slots):
            self.copy(self.shift(i), self.boson, *slots).start()
        now = (start, size)
        pack(0, now)
        def one(i):
            pack(i, now)
            send(i - 1, now)
        loop(1, self.n - 3, one)
        waiting = functools.partial(send, self.n - 4, now)
        if behind[1] > 0:
            for i in (self.n - 3, self.n - 2):
                pack(i, behind)
                waiting()
                waiting = functools.partial(send, i, behind)
        return waiting

    def keep(self, tiles, table):
        self.pack(self.incoming, self.boson, tiles, table, 0, self.capacity)

    def received(self):
        loop(1, self.n, lambda s: self.copy(s, (self.boson + self.n - s) % self.n).wait_recv())

    def sent(self):
        loop(1, self.n, lambda s: self.copy(s, self.boson).wait_send())


class Greeting:
    def __init__(self, block_peers, boson_peers):
        self.barrier = pltpu.get_barrier_semaphore()
        boson, block = lax.axis_index("boson"), lax.axis_index("block")
        self.peers = [(boson, peer) for peer in block_peers] + [(peer, block) for peer in boson_peers]

    def say(self):
        for peer in self.peers:
            pl.semaphore_signal(self.barrier, inc=1, device_id=peer, device_id_type=MESH)

    def hear(self):
        pl.semaphore_wait(self.barrier, len(self.peers))


class Plan:
    def __init__(self, *runs):
        self.runs = runs

    def due(self):
        chunk = slot = 0
        for times, chunks, slots in self.runs:
            for _ in range(times):
                chunk, slot = chunk + chunks, slot + slots
                yield chunk, slot


def plans(chunks, lag):
    ahead = Plan((1, lag + 1, 1), (chunks - lag - 1, 1, 1))
    return ahead, Plan((1, lag + 1, 1), ((chunks - lag - 2) // 2, 2, 2))


def bits(count):
    return count.bit_length() - 1


class Items:
    def __init__(self, nboson, targets, first_row, row_tiles):
        _, col_blocks, count = targets.shape
        points, per_point = count // nboson, row_tiles * col_blocks
        self.total, self.chunks, self.pair = points * per_point, points * PARTS, col_blocks // PARTS
        self.row_tiles = row_tiles
        boson = lax.axis_index("boson")
        flat = targets[pl.ds(first_row, row_tiles)].reshape(per_point, count)
        lane = lax.broadcasted_iota(jnp.int32, flat.shape, 1)
        own = jnp.concatenate(
            [jnp.sum(jnp.where(lane == boson * points + q, flat, 0), axis=1, keepdims=True)
             for q in range(points)], axis=0)
        self.item = lax.broadcasted_iota(jnp.int32, (self.total, 1), 0)
        self.shift = ((own >> bits(points)) - boson) & (nboson - 1)
        self.row = (self.item >> bits(col_blocks)) & (row_tiles - 1)
        self.column = self.item & (col_blocks - 1)
        self.target = (own & (points - 1)) * per_point + (self.item & (per_point - 1))
        part = self.column >> bits(self.pair)
        self.ahead = (self.item >> bits(per_point)) * PARTS + part
        self.home = (own & (points - 1)) * PARTS + part

    def spread(self, keys, values, width):
        wanted = lax.broadcasted_iota(jnp.int32, (self.total, width), 1)
        return jnp.sum(jnp.where(keys == wanted, values, 0), axis=0, keepdims=True)

    def tile(self, chunk, places):
        if places is not None:
            lane = lax.broadcasted_iota(jnp.int32, (self.total, places.shape[1]), 1)
            chunk = jnp.sum(jnp.where(chunk == lane, places, 0), axis=1, keepdims=True)
        return (chunk * self.row_tiles + self.row) * self.pair + (self.column & (self.pair - 1))


def slot_tables(nboson, capacity, items, ahead_places, home_places, rows):
    boson = lax.axis_index("boson")
    same = items.spread(items.item, items.shift, items.total) == items.shift
    def rank(key):
        later = same & (items.spread(items.item, key, items.total) > key)
        return capacity - 1 - jnp.sum(jnp.where(later, 1, 0), axis=1, keepdims=True)

    there = ((boson + items.shift) & (nboson - 1)) * capacity
    here = ((boson - items.shift) & (nboson - 1)) * capacity
    ahead = items.tile(items.ahead, ahead_places)
    home = items.tile(items.home, home_places)
    out_rank, back_rank = rank(ahead), rank(home)
    width = rows.shape[0] // 8 * rows.shape[1]
    last_slot, last_item = nboson * capacity - 1, items.total - 1
    for k, (keys, values, last) in enumerate((
            (items.item, there + back_rank, last_slot), (there + out_rank, ahead, last_item),
            (items.target, here + out_rank, last_slot), (here + back_rank, home, last_item))):
        line = jnp.clip(items.spread(keys, values, width), 0, last)
        for h in range(width // LANES):
            rows[h * 8 + k:h * 8 + k + 1, :] = line[:, h * LANES:(h + 1) * LANES]


def choose_orders(nboson, nblock, capacity, fixed, plans, targets, row_tiles, rows):
    def counts(pick, items_of):
        total = 0.
        for b, items in enumerate(items_of):
            lane = lax.broadcasted_iota(jnp.int32, (items.total, LANES), 1)
            hot = jnp.where(lane == b * nboson + items.shift, 1., 0.).astype(jnp.bfloat16)
            chunk = items.spread(items.item, pick(items), items.total)
            turn = lax.broadcasted_iota(jnp.int32, (items.chunks, items.total), 0)
            member = jnp.where(chunk == turn, 1., 0.).astype(jnp.bfloat16)
            total = total + jnp.dot(member, hot, preferred_element_type=jnp.float32)
        return total

    items_of = [Items(nboson, targets, b * row_tiles, row_tiles) for b in range(nblock)]
    chunks = items_of[0].chunks
    lane = lax.broadcasted_iota(jnp.int32, (1, LANES), 1)
    weighed = (lane < nboson * nblock) & ((lane & (nboson - 1)) > 0)
    chunk = lax.broadcasted_iota(jnp.int32, (chunks, 1), 0)
    shift = lane & (nboson - 1)
    behind = jnp.where((shift == 1) | (shift == nboson - 1), 1., 0.)
    tables, begin = [], []
    for pick, held in zip((lambda i: i.ahead, lambda i: i.home), fixed):
        count = counts(pick, items_of)
        gain = jnp.exp(-2. * jnp.minimum(count, 30.))
        spare = capacity - jnp.sum(count, axis=0, keepdims=True) + behind
        ready = spare + jnp.sum(jnp.where(chunk < held, count, 0.), axis=0, keepdims=True)
        tables.append((count, gain, spare))
        begin.append((jnp.where(weighed, jnp.exp(-2. * jnp.clip(ready, -30., 30.)), 0.),
                      jnp.broadcast_to(jnp.where(chunk < held, chunk, -1), (chunks, LANES))))

    def choose(t, state, held=(0, 0)):
        out = []
        for (weight, turn), (_, gain, _), first in zip(state, tables, held):
            if isinstance(t, int) and t < first:
                out.append((weight, turn))
                continue
            score = jnp.sum(weight * gain, axis=1, keepdims=True)
            score = jnp.where(turn < 0, score, jnp.inf)
            best = jnp.min(score, axis=0, keepdims=True)
            index = lax.broadcasted_iota(jnp.int32, score.shape, 0)
            hit = index == jnp.min(jnp.where(score == best, index, chunks), axis=0, keepdims=True)
            weight = weight * jnp.sum(jnp.where(hit, gain, 0.), axis=0, keepdims=True)
            out.append((weight, jnp.where(hit, t, turn)))
        return tuple(out)

    state = tuple(begin)
    for held in range(min(fixed), max(fixed)):
        state = choose(held, state, fixed)
    chosen = lax.fori_loop(max(fixed), chunks, choose, state)
    late = jnp.zeros((1, LANES), jnp.float32)
    turns = []
    for k, ((_, turn), (count, _, spare), plan) in enumerate(zip(chosen, tables, plans)):
        index = lax.broadcasted_iota(jnp.int32, turn.shape, 0)
        column = lax.broadcasted_iota(jnp.int32, turn.shape, 1)
        order = jnp.sum(jnp.where(turn == column, index, 0), axis=0, keepdims=True)
        rows[k:k + 1, :] = jnp.clip(order, 0, chunks - 1)
        turned = jnp.sum(jnp.where(index == column, turn, 0), axis=0, keepdims=True)
        turns.append(jnp.clip(turned, 0, chunks - 1))
        rows[k + 2:k + 3, :] = turns[k]
        for done, slots in plan.due():
            ready = jnp.sum(jnp.where(turn < done, count, 0.), axis=0, keepdims=True)
            late = late + jnp.where(weighed & (ready + spare < slots), 1., 0.)
    return turns, jnp.sum(late, axis=1, keepdims=True)


class Table:
    def __init__(self, ref, k):
        self.ref, self.k = ref, k

    def __getitem__(self, i):
        return self.ref[i // LANES * 8 + self.k, i % LANES]


def kernel(nboson, nblock, row_tiles, col_blocks, lag, *refs):
    relabel, gamma_in, full_in, chi_ph, pp_in, chi_pp, out, *refs = refs
    early = lag is not None
    late, refs = (refs[0], refs[1:]) if early else (None, refs)
    (full, pp, full_blocks, pp_blocks, gamma, scaled, base, tiles, packed, landed, back, returned,
     targets, table_rows, table, order_rows, orders,
     gamma_sem, table_sem, ahead_s, ahead_r, home_s, home_r, *gather_sems) = refs
    half = len(gather_sems) // 2
    chunks = full.shape[0]
    fixed, free = (FIXED, 0) if early else (chunks, chunks)
    first = Gather(nblock, full_in, full_blocks, full, fixed, gather_sems[:half])
    second = Gather(nblock, pp_in, pp_blocks, pp, free, gather_sems[half:])
    ahead_plan, home_plan = plans(chunks, lag) if early else (Plan(), Plan())
    ahead = Exchange(nboson, packed, landed, ahead_s, ahead_r)
    home = Exchange(nboson, back, returned, home_s, home_r)
    points, rows, order = gamma.shape
    high, wide = rows // row_tiles, order // col_blocks
    pair = first.cols // wide
    capacity = landed.shape[1]
    send_slot, item_of, back_slot, back_item_of = (Table(table, i) for i in range(4))
    load_targets = pltpu.make_async_copy(relabel, targets, table_sem.at[0])
    load_table = pltpu.make_async_copy(table_rows, table, table_sem.at[1])
    load_gamma = pltpu.make_async_copy(gamma_in, gamma, gamma_sem)

    greeting = Greeting(first.peers(), ahead.peers())
    greeting.say()
    load_targets.start()
    for g in range(fixed):
        first.load(g).start()
    greeting.hear()
    for g in range(fixed):
        first.load(g).wait()
    first.start_far(0, fixed)
    for g in range(fixed, chunks):
        first.load(g).start()
    first.start_near(0, fixed)
    load_gamma.start()
    load_targets.wait()
    if early:
        turns, count = choose_orders(
            nboson, nblock, capacity, (fixed, free), (ahead_plan, home_plan), targets, row_tiles,
            order_rows)
        load_orders = pltpu.make_async_copy(order_rows, orders, table_sem.at[2])
        load_orders.start()
        late[...] = jnp.broadcast_to(count, late.shape)
        for g in range(fixed, chunks):
            first.load(g).wait()
        load_orders.wait()
        first.pack(lambda g: orders[0, g])
        first.start_far(fixed, chunks)
    else:
        turns = None, None

    for g in range(chunks):
        second.load(g).start()
    items = Items(nboson, targets, lax.axis_index("block") * row_tiles, row_tiles)
    slot_tables(nboson, capacity, items, *turns, table_rows)
    if early:
        first.start_near(fixed, chunks)
    load_table.start()
    load_gamma.wait()
    for q in range(points):
        scaled[q] = (gamma[q].astype(jnp.float32) * chi_ph[q:q + 1, :]).astype(jnp.bfloat16)
    load_table.wait()

    def product(gather, g, k):
        point = (orders[k, g] if early else g) // PARTS
        phi = jnp.dot(scaled[point], gather.whole[g], preferred_element_type=jnp.float32)
        wire = phi.astype(jnp.bfloat16)
        for r in range(row_tiles):
            for i in range(pair):
                tiles[(g * row_tiles + r) * pair + i] = (
                    wire[r * high:(r + 1) * high, i * wide:(i + 1) * wide])
        return phi

    def staged(exchange, table, plan, step):
        chunk = slot = 0
        for times, span, slots in plan.runs:
            def one(i, chunk=chunk, slot=slot, span=span, slots=slots):
                begin = chunk + i * span
                loop(begin, begin + span, step)
                exchange.part(tiles, table, slot + i * slots, slots, first=slot == 0)()
            one(0) if times == 1 else loop(0, times, one)
            chunk, slot = chunk + times * span, slot + times * slots
        loop(chunk, chunks, step)
        last = exchange.part(tiles, table, slot, capacity - slot, first=slot == 0, last=True)
        exchange.keep(tiles, table)
        last()

    def ahead_step(g):
        @pl.when(g == chunks - 3)
        def _():
            for i in range(chunks):
                second.load(i).wait()
            if early:
                second.pack(lambda i: orders[1, i])
        @pl.when(g == chunks - 1)
        def _():
            first.left(chunks - 1)
            second.start_far(0, chunks)
        first.relay(g)
        first.arrived(g)
        base[g] = product(first, g, 0)

    staged(ahead, item_of, ahead_plan, ahead_step)
    second.start_near(0, chunks)
    first.sent(0, chunks - 1)
    waiting = chunks // 4
    loop(0, waiting, second.relay)
    ahead.received()

    flat = landed.reshape(nboson * capacity, high, wide)
    def unpack(p):
        chi = chi_pp[pl.ds(p, 1), :]
        for c in range(col_blocks):
            for r in range(row_tiles):
                tile = flat[back_slot[(p * row_tiles + r) * col_blocks + c]]
                scaled[p, r * high:(r + 1) * high, c * wide:(c + 1) * wide] = (
                    tile.astype(jnp.float32) * chi[:, c * wide:(c + 1) * wide]).astype(jnp.bfloat16)
    loop(0, points, unpack)

    def home_step(g):
        @pl.when(g >= waiting)
        def _():
            second.relay(g)
        second.arrived(g)
        product(second, g, 1)

    staged(home, back_item_of, home_plan, home_step)
    ahead.sent()
    second.sent(0, chunks)
    home.received()

    flat_back = returned.reshape(nboson * capacity, high, wide)
    def finish(q):
        for c in range(col_blocks):
            chunk = q * PARTS + c // pair
            turn = orders[2, chunk] if early else chunk
            for r in range(row_tiles):
                tile = flat_back[send_slot[(q * row_tiles + r) * col_blocks + c]]
                at = (q, slice(r * high, (r + 1) * high), slice(c * wide, (c + 1) * wide))
                phi = base[turn, r * high:(r + 1) * high, c % pair * wide:(c % pair + 1) * wide]
                total = gamma[at].astype(jnp.float32) + phi + tile.astype(jnp.float32)
                out[at] = total.astype(jnp.bfloat16)
    loop(0, points, finish)
    home.sent()


def local(nboson, nblock, gamma_ph, full_ph, chi_ph, pp_vertex, chi_pp, relabel):
    points, rows, order = gamma_ph.shape
    row_tiles, col_blocks = relabel.shape[1] // nblock, relabel.shape[2]
    high, wide = rows // row_tiles, order // col_blocks
    total = points * row_tiles * col_blocks
    capacity = -(-total // nboson) + 1
    bf16, f32 = jnp.bfloat16, jnp.float32
    chunks, cols = points * PARTS, order // PARTS
    whole = pltpu.VMEM((chunks, order, cols), bf16)
    blocks = pltpu.VMEM((chunks, rows, cols), bf16)
    shard = pltpu.VMEM(gamma_ph.shape, bf16)
    slabs = pltpu.VMEM((nboson, capacity, high, wide), bf16)
    table_rows = -(-(nboson * capacity) // LANES) * 8
    for count in (nboson, points, row_tiles * col_blocks, col_blocks, PARTS):
        assert count & (count - 1) == 0
    vmem = pl.BlockSpec(memory_space=pltpu.VMEM)
    hbm = pl.BlockSpec(memory_space=pl.ANY)
    operands = (relabel.transpose(1, 2, 0), gamma_ph, full_ph, chi_ph, pp_vertex, chi_pp)

    def window(lag):
        result = pltpu.VMEM(gamma_ph.shape, bf16)
        early = lag is not None
        return pl.pallas_call(
            functools.partial(kernel, nboson, nblock, row_tiles, col_blocks, lag),
            out_shape=(result, pltpu.VMEM((8, LANES), jnp.float32)) if early else result,
            name="early" if early else "plain",
            in_specs=[hbm, hbm, hbm, vmem, hbm, vmem], out_specs=(vmem, vmem) if early else vmem,
            scratch_shapes=[
                whole, whole, blocks, blocks, shard, shard, pltpu.VMEM((chunks, rows, cols), f32),
                pltpu.VMEM((total, high, wide), bf16), slabs, slabs, slabs, slabs,
                pltpu.VMEM(operands[0].shape, jnp.int32),
                pltpu.VMEM((table_rows, LANES), jnp.int32), pltpu.SMEM((table_rows, LANES), jnp.int32),
                pltpu.VMEM((8, LANES), jnp.int32), pltpu.SMEM((8, LANES), jnp.int32),
                DMA, DMA((3,)), DMA((nboson,)), DMA((nboson,)), DMA((nboson,)), DMA((nboson,)),
            ] + gather_scratch(nblock, points) + gather_scratch(nblock, points),
            compiler_params=pltpu.CompilerParams(
                collective_id=int(early), has_side_effects=True, vmem_limit_bytes=60 * 1024 * 1024),
        )(*operands)

    if capacity <= chunks - LAG or nboson * nblock > LANES:
        return window(None)
    result, late = window(LAG)
    return lax.cond(late[0, 0] == 0, lambda: result, lambda: window(None))


def solution(mesh):
    placed = (
        P("boson", "block", None),
        P("boson", "block", None),
        P("boson", None),
        P("boson", "block", None),
        P("boson", None),
        P(),
    )
    return jax.shard_map(
        functools.partial(local, mesh.shape["boson"], mesh.shape["block"]), mesh=mesh,
        in_specs=placed, out_specs=P("boson", "block", None), check_vma=False,
    )
```

```python
import functools
import jax
import jax.numpy as jnp
from jax import lax
from jax.experimental import pallas as pl
from jax.experimental.pallas import tpu as pltpu
from jax.sharding import PartitionSpec as P

MESH = pl.DeviceIdType.MESH
DMA = pltpu.SemaphoreType.DMA
PARTS = 4
FIXED = 2
LAG = 2
LANES = 128


def loop(start, stop, body):
    lax.fori_loop(start, stop, lambda i, carry: (body(i), carry)[1], 0)


class Gather:
    def __init__(self, nblock, shard, blocks, whole, fixed, sems):
        self.nblock, self.shard, self.blocks, self.whole = nblock, shard, blocks, whole
        self.far_s, self.far_r, self.near_s, self.near_r, self.fwd_s, self.fwd_r, self.loc = sems
        self.chunks, _, self.cols = whole.shape
        self.rows = shard.shape[1]
        self.fixed = fixed
        self.boson = lax.axis_index("boson")
        self.here = lax.axis_index("block")
        self.partner = self.here + 1 - 2 * (self.here % 2)

    def peers(self):
        out = [self.partner]
        for j in range(1, self.nblock // 2):
            out.append((self.here + 2 * j) % self.nblock)
        return out

    def place(self, g, owner):
        rows = pl.ds(pl.multiple_of(owner * self.rows, self.rows), self.rows)
        return self.whole.at[g, rows]

    def load(self, g):
        source = self.shard.at[g // PARTS, :, g % PARTS * self.cols:(g % PARTS + 1) * self.cols]
        target = self.place(g, self.here) if g < self.fixed else self.blocks.at[g]
        return pltpu.make_async_copy(source, target, self.loc.at[g])

    def pack(self, order):
        def one(g):
            self.place(g, self.here)[...] = self.blocks[order(g)]
        loop(self.fixed, self.chunks, one)

    def far(self, g, j, owner):
        return pltpu.make_async_remote_copy(
            src_ref=self.place(g, owner), dst_ref=self.place(g, owner),
            send_sem=self.far_s.at[j - 1, g], recv_sem=self.far_r.at[j - 1, g],
            device_id=(self.boson, (self.here + 2 * j) % self.nblock), device_id_type=MESH)

    def near(self, g, owner):
        return pltpu.make_async_remote_copy(
            src_ref=self.place(g, owner), dst_ref=self.place(g, owner),
            send_sem=self.near_s.at[g], recv_sem=self.near_r.at[g],
            device_id=(self.boson, self.partner), device_id_type=MESH)

    def forward(self, g, j, owner):
        return pltpu.make_async_remote_copy(
            src_ref=self.place(g, owner), dst_ref=self.place(g, owner),
            send_sem=self.fwd_s.at[j - 1, g], recv_sem=self.fwd_r.at[j - 1, g],
            device_id=(self.boson, self.partner), device_id_type=MESH)

    def each_far(self, act):
        for j in range(1, self.nblock // 2):
            act(j)

    def start_far(self, begin, end):
        loop(begin, end, lambda g: self.each_far(lambda j: self.far(g, j, self.here).start()))

    def start_near(self, begin, end):
        loop(begin, end, lambda g: self.near(g, self.here).start())

    def relay(self, g):
        def one(j):
            owner = (self.here + self.nblock - 2 * j) % self.nblock
            self.far(g, j, owner).wait_recv()
            self.forward(g, j, owner).start()
        self.each_far(one)

    def arrived(self, g):
        self.near(g, self.partner).wait_recv()
        def one(j):
            twin = (self.partner + self.nblock - 2 * j) % self.nblock
            self.forward(g, j, twin).wait_recv()
        self.each_far(one)

    def left(self, g):
        self.each_far(lambda j: self.far(g, j, self.here).wait_send())

    def sent(self, begin, end):
        loop(begin, end, self.left)
        def one(g):
            self.near(g, self.here).wait_send()
            def fwd(j):
                owner = (self.here + self.nblock - 2 * j) % self.nblock
                self.forward(g, j, owner).wait_send()
            self.each_far(fwd)
        loop(0, self.chunks, one)


def gather_scratch(nblock, points):
    far, chunks = max(nblock // 2 - 1, 1), points * PARTS
    return [DMA((far, chunks)), DMA((far, chunks)), DMA((chunks,)), DMA((chunks,)),
            DMA((far, chunks)), DMA((far, chunks)), DMA((chunks,))]


class Exchange:
    def __init__(self, nboson, outgoing, incoming, send, recv):
        self.n, self.outgoing, self.incoming = nboson, outgoing, incoming
        self.send, self.recv = send, recv
        self.capacity = outgoing.shape[1]
        self.boson = lax.axis_index("boson")
        self.block = lax.axis_index("block")

    def shift(self, i):
        return self.n // 2 + (1 - 2 * (i % 2)) * ((i + 1) // 2)

    def copy(self, s, slot, start=0, size=None):
        dest = (self.boson + s) % self.n
        slots = pl.ds(start, self.capacity if size is None else size)
        return pltpu.make_async_remote_copy(
            src_ref=self.outgoing.at[dest, slots], dst_ref=self.incoming.at[slot, slots],
            send_sem=self.send.at[s], recv_sem=self.recv.at[s],
            device_id=(dest, self.block), device_id_type=MESH)

    def pack(self, target, dest, tiles, table, start, size):
        for k in range(size):
            target[dest, start + k] = tiles[table[dest * self.capacity + start + k]]

    def part(self, tiles, table, start, size, first=False, last=False):
        behind = (start if first else start - 1, size - first + last)
        def pack(i, slots):
            dest = (self.boson + self.shift(i)) % self.n
            self.pack(self.outgoing, dest, tiles, table, *slots)
        def send(i, slots):
            self.copy(self.shift(i), self.boson, *slots).start()
        now = (start, size)
        pack(0, now)
        def one(i):
            pack(i, now)
            send(i - 1, now)
        loop(1, self.n - 3, one)
        waiting = functools.partial(send, self.n - 4, now)
        if behind[1] > 0:
            for i in (self.n - 3, self.n - 2):
                pack(i, behind)
                waiting()
                waiting = functools.partial(send, i, behind)
        return waiting

    def keep(self, tiles, table):
        self.pack(self.incoming, self.boson, tiles, table, 0, self.capacity)

    def received(self):
        loop(1, self.n, lambda s: self.copy(s, (self.boson + self.n - s) % self.n).wait_recv())

    def sent(self):
        loop(1, self.n, lambda s: self.copy(s, self.boson).wait_send())


class Greeting:
    def __init__(self, nboson, block_peers, met):
        self.barrier, self.met = pltpu.get_barrier_semaphore(), met
        boson, block = lax.axis_index("boson"), lax.axis_index("block")
        self.pairs = [(boson + (1 - 2 * (boson // 2 ** bit % 2)) * 2 ** bit, block)
                      for bit in range(bits(nboson))]
        self.peers = [(boson, peer) for peer in block_peers] + self.pairs

    def say(self):
        for peer in self.peers:
            pl.semaphore_signal(self.barrier, inc=1, device_id=peer, device_id_type=MESH)

    def hear(self):
        pl.semaphore_wait(self.barrier, len(self.peers))

    def tell(self, bit):
        pl.semaphore_signal(self.met.at[bit], inc=1, device_id=self.pairs[bit], device_id_type=MESH)

    def pass_on(self, bit):
        pl.semaphore_wait(self.met.at[bit], 1)
        if bit + 1 < len(self.pairs):
            self.tell(bit + 1)


class Plan:
    def __init__(self, *runs):
        self.runs = runs

    def due(self):
        chunk = slot = 0
        for times, chunks, slots in self.runs:
            for _ in range(times):
                chunk, slot = chunk + chunks, slot + slots
                yield chunk, slot


def plans(chunks, lag):
    ahead = Plan((1, lag + 1, 1), (chunks - lag - 1, 1, 1))
    return ahead, Plan((1, lag + 1, 1), ((chunks - lag - 2) // 2, 2, 2))


def bits(count):
    return count.bit_length() - 1


class Items:
    def __init__(self, nboson, targets, first_row, row_tiles, boson=None):
        _, col_blocks, count = targets.shape
        points, per_point = count // nboson, row_tiles * col_blocks
        self.total, self.chunks, self.pair = points * per_point, points * PARTS, col_blocks // PARTS
        self.row_tiles = row_tiles
        flat = targets[pl.ds(first_row, row_tiles)].reshape(per_point, count)
        lane = lax.broadcasted_iota(jnp.int32, flat.shape, 1)
        own = jnp.concatenate(
            [flat[:, q:q + 1] if boson is None else
             jnp.sum(jnp.where(lane == boson * points + q, flat, 0), axis=1, keepdims=True)
             for q in range(points)], axis=0)
        self.item = lax.broadcasted_iota(jnp.int32, (self.total, 1), 0)
        self.shift = ((own >> bits(points)) - (0 if boson is None else boson)) & (nboson - 1)
        self.row = (self.item >> bits(col_blocks)) & (row_tiles - 1)
        self.column = self.item & (col_blocks - 1)
        self.target = (own & (points - 1)) * per_point + (self.item & (per_point - 1))
        part = self.column >> bits(self.pair)
        self.ahead = (self.item >> bits(per_point)) * PARTS + part
        self.home = (own & (points - 1)) * PARTS + part

    def spread(self, keys, values, width):
        wanted = lax.broadcasted_iota(jnp.int32, (self.total, width), 1)
        return jnp.sum(jnp.where(keys == wanted, values, 0), axis=0, keepdims=True)

    def tile(self, chunk, places):
        if places is not None:
            lane = lax.broadcasted_iota(jnp.int32, (self.total, places.shape[1]), 1)
            chunk = jnp.sum(jnp.where(chunk == lane, places, 0), axis=1, keepdims=True)
        return (chunk * self.row_tiles + self.row) * self.pair + (self.column & (self.pair - 1))


def slot_tables(nboson, capacity, items, ahead_places, home_places, rows):
    boson = lax.axis_index("boson")
    same = items.spread(items.item, items.shift, items.total) == items.shift
    def rank(key):
        later = same & (items.spread(items.item, key, items.total) > key)
        return capacity - 1 - jnp.sum(jnp.where(later, 1, 0), axis=1, keepdims=True)

    there = ((boson + items.shift) & (nboson - 1)) * capacity
    here = ((boson - items.shift) & (nboson - 1)) * capacity
    ahead = items.tile(items.ahead, ahead_places)
    home = items.tile(items.home, home_places)
    out_rank, back_rank = rank(ahead), rank(home)
    width = rows.shape[0] // 8 * rows.shape[1]
    last_slot, last_item = nboson * capacity - 1, items.total - 1
    for k, (keys, values, last) in enumerate((
            (items.item, there + back_rank, last_slot), (there + out_rank, ahead, last_item),
            (items.target, here + out_rank, last_slot), (here + back_rank, home, last_item))):
        line = jnp.clip(items.spread(keys, values, width), 0, last)
        for h in range(width // LANES):
            rows[h * 8 + k:h * 8 + k + 1, :] = line[:, h * LANES:(h + 1) * LANES]


def choose_orders(nboson, nblock, capacity, fixed, plans, targets, row_tiles, rows):
    def counts(pick, items_of):
        total = 0.
        for b, items in enumerate(items_of):
            lane = lax.broadcasted_iota(jnp.int32, (items.total, LANES), 1)
            hot = jnp.where(lane == b * nboson + items.shift, 1., 0.).astype(jnp.bfloat16)
            chunk = items.spread(items.item, pick(items), items.total)
            turn = lax.broadcasted_iota(jnp.int32, (items.chunks, items.total), 0)
            member = jnp.where(chunk == turn, 1., 0.).astype(jnp.bfloat16)
            total = total + jnp.dot(member, hot, preferred_element_type=jnp.float32)
        return total

    items_of = [Items(nboson, targets, b * row_tiles, row_tiles) for b in range(nblock)]
    chunks = items_of[0].chunks
    lane = lax.broadcasted_iota(jnp.int32, (1, LANES), 1)
    weighed = (lane < nboson * nblock) & ((lane & (nboson - 1)) > 0)
    chunk = lax.broadcasted_iota(jnp.int32, (chunks, 1), 0)
    shift = lane & (nboson - 1)
    behind = jnp.where((shift == 1) | (shift == nboson - 1), 1., 0.)
    tables, begin = [], []
    for pick, held in zip((lambda i: i.ahead, lambda i: i.home), fixed):
        count = counts(pick, items_of)
        gain = jnp.exp(-2. * jnp.minimum(count, 30.))
        spare = capacity - jnp.sum(count, axis=0, keepdims=True) + behind
        ready = spare + jnp.sum(jnp.where(chunk < held, count, 0.), axis=0, keepdims=True)
        tables.append((count, gain, spare))
        begin.append((jnp.where(weighed, jnp.exp(-2. * jnp.clip(ready, -30., 30.)), 0.),
                      jnp.broadcast_to(jnp.where(chunk < held, chunk, -1), (chunks, LANES))))

    def choose(t, state, held=(0, 0)):
        out = []
        for (weight, turn), (_, gain, _), first in zip(state, tables, held):
            if isinstance(t, int) and t < first:
                out.append((weight, turn))
                continue
            score = jnp.sum(weight * gain, axis=1, keepdims=True)
            score = jnp.where(turn < 0, score, jnp.inf)
            best = jnp.min(score, axis=0, keepdims=True)
            index = lax.broadcasted_iota(jnp.int32, score.shape, 0)
            hit = index == jnp.min(jnp.where(score == best, index, chunks), axis=0, keepdims=True)
            weight = weight * jnp.sum(jnp.where(hit, gain, 0.), axis=0, keepdims=True)
            out.append((weight, jnp.where(hit, t, turn)))
        return tuple(out)

    state = tuple(begin)
    for held in range(min(fixed), max(fixed)):
        state = choose(held, state, fixed)
    chosen = lax.fori_loop(max(fixed), chunks, choose, state)
    late = jnp.zeros((1, LANES), jnp.float32)
    turns = []
    for k, ((_, turn), (count, _, spare), plan) in enumerate(zip(chosen, tables, plans)):
        index = lax.broadcasted_iota(jnp.int32, turn.shape, 0)
        column = lax.broadcasted_iota(jnp.int32, turn.shape, 1)
        order = jnp.sum(jnp.where(turn == column, index, 0), axis=0, keepdims=True)
        rows[k:k + 1, :] = jnp.clip(order, 0, chunks - 1)
        turned = jnp.sum(jnp.where(index == column, turn, 0), axis=0, keepdims=True)
        turns.append(jnp.clip(turned, 0, chunks - 1))
        rows[k + 2:k + 3, :] = turns[k]
        for done, slots in plan.due():
            ready = jnp.sum(jnp.where(turn < done, count, 0.), axis=0, keepdims=True)
            late = late + jnp.where(weighed & (ready + spare < slots), 1., 0.)
    return turns, jnp.sum(late, axis=1, keepdims=True)


class Table:
    def __init__(self, ref, k):
        self.ref, self.k = ref, k

    def __getitem__(self, i):
        return self.ref[i // LANES * 8 + self.k, i % LANES]


def kernel(nboson, nblock, row_tiles, col_blocks, lag, *refs):
    relabel, gamma_in, full_in, chi_ph, pp_in, chi_pp, out, *refs = refs
    early = lag is not None
    late, refs = (refs[0], refs[1:]) if early else (None, refs)
    (full, pp, full_blocks, pp_blocks, gamma, scaled, base, tiles, packed, landed, back, returned,
     targets, table_rows, table, order_rows, orders,
     gamma_sem, table_sem, met, ahead_s, ahead_r, home_s, home_r, *gather_sems) = refs
    half = len(gather_sems) // 2
    chunks = full.shape[0]
    fixed, free = (FIXED, 0) if early else (chunks, chunks)
    first = Gather(nblock, full_in, full_blocks, full, fixed, gather_sems[:half])
    second = Gather(nblock, pp_in, pp_blocks, pp, free, gather_sems[half:])
    ahead_plan, home_plan = plans(chunks, lag) if early else (Plan(), Plan())
    ahead = Exchange(nboson, packed, landed, ahead_s, ahead_r)
    home = Exchange(nboson, back, returned, home_s, home_r)
    points, rows, order = gamma.shape
    high, wide = rows // row_tiles, order // col_blocks
    pair = first.cols // wide
    capacity = landed.shape[1]
    send_slot, item_of, back_slot, back_item_of = (Table(table, i) for i in range(4))
    load_targets = pltpu.make_async_copy(relabel, targets, table_sem.at[0])
    load_table = pltpu.make_async_copy(table_rows, table, table_sem.at[1])
    load_gamma = pltpu.make_async_copy(gamma_in, gamma, gamma_sem)

    greeting = Greeting(nboson, first.peers(), met)
    greeting.say()
    load_targets.start()
    for g in range(fixed):
        first.load(g).start()
    greeting.hear()
    for g in range(fixed):
        first.load(g).wait()
    first.start_far(0, fixed)
    greeting.tell(0)
    for g in range(fixed, chunks):
        first.load(g).start()
    first.start_near(0, fixed)
    load_gamma.start()
    load_targets.wait()
    if early:
        turns, count = choose_orders(
            nboson, nblock, capacity, (fixed, free), (ahead_plan, home_plan), targets, row_tiles,
            order_rows)
        load_orders = pltpu.make_async_copy(order_rows, orders, table_sem.at[2])
        load_orders.start()
        late[0, 0] = jnp.where(jnp.sum(count) > 0, 1, 0)
        for g in range(fixed, chunks):
            first.load(g).wait()
        load_orders.wait()
        first.pack(lambda g: orders[0, g])
        first.start_far(fixed, chunks)
    else:
        turns = None, None

    for g in range(chunks):
        second.load(g).start()
    items = Items(nboson, targets, lax.axis_index("block") * row_tiles, row_tiles,
                  lax.axis_index("boson"))
    slot_tables(nboson, capacity, items, *turns, table_rows)
    if early:
        first.start_near(fixed, chunks)
    load_table.start()
    for bit in range(bits(nboson)):
        greeting.pass_on(bit)
    load_gamma.wait()
    for q in range(points):
        scaled[q] = (gamma[q].astype(jnp.float32) * chi_ph[q:q + 1, :]).astype(jnp.bfloat16)
    load_table.wait()

    def product(gather, g, k):
        point = (orders[k, g] if early else g) // PARTS
        phi = jnp.dot(scaled[point], gather.whole[g], preferred_element_type=jnp.float32)
        wire = phi.astype(jnp.bfloat16)
        for r in range(row_tiles):
            for i in range(pair):
                tiles[(g * row_tiles + r) * pair + i] = (
                    wire[r * high:(r + 1) * high, i * wide:(i + 1) * wide])
        return phi

    def staged(exchange, table, plan, step):
        chunk = slot = 0
        for times, span, slots in plan.runs:
            def one(i, chunk=chunk, slot=slot, span=span, slots=slots):
                begin = chunk + i * span
                loop(begin, begin + span, step)
                exchange.part(tiles, table, slot + i * slots, slots, first=slot == 0)()
            one(0) if times == 1 else loop(0, times, one)
            chunk, slot = chunk + times * span, slot + times * slots
        loop(chunk, chunks, step)
        last = exchange.part(tiles, table, slot, capacity - slot, first=slot == 0, last=True)
        exchange.keep(tiles, table)
        last()

    def ahead_step(g):
        @pl.when(g == chunks - 3)
        def _():
            for i in range(chunks):
                second.load(i).wait()
            if early:
                second.pack(lambda i: orders[1, i])
        @pl.when(g == chunks - 1)
        def _():
            first.left(chunks - 1)
            second.start_far(0, chunks)
        first.relay(g)
        first.arrived(g)
        base[g] = product(first, g, 0)

    staged(ahead, item_of, ahead_plan, ahead_step)
    second.start_near(0, chunks)
    first.sent(0, chunks - 1)
    waiting = chunks // 4
    loop(0, waiting, second.relay)
    ahead.received()

    flat = landed.reshape(nboson * capacity, high, wide)
    def unpack(p):
        chi = chi_pp[pl.ds(p, 1), :]
        for c in range(col_blocks):
            for r in range(row_tiles):
                tile = flat[back_slot[(p * row_tiles + r) * col_blocks + c]]
                scaled[p, r * high:(r + 1) * high, c * wide:(c + 1) * wide] = (
                    tile.astype(jnp.float32) * chi[:, c * wide:(c + 1) * wide]).astype(jnp.bfloat16)
    loop(0, points, unpack)

    def home_step(g):
        @pl.when(g >= waiting)
        def _():
            second.relay(g)
        second.arrived(g)
        product(second, g, 1)

    staged(home, back_item_of, home_plan, home_step)
    ahead.sent()
    second.sent(0, chunks)
    home.received()

    flat_back = returned.reshape(nboson * capacity, high, wide)
    def finish(q):
        for c in range(col_blocks):
            chunk = q * PARTS + c // pair
            turn = orders[2, chunk] if early else chunk
            for r in range(row_tiles):
                tile = flat_back[send_slot[(q * row_tiles + r) * col_blocks + c]]
                at = (q, slice(r * high, (r + 1) * high), slice(c * wide, (c + 1) * wide))
                phi = base[turn, r * high:(r + 1) * high, c % pair * wide:(c % pair + 1) * wide]
                total = gamma[at].astype(jnp.float32) + phi + tile.astype(jnp.float32)
                out[at] = total.astype(jnp.bfloat16)
    loop(0, points, finish)
    home.sent()


def local(nboson, nblock, gamma_ph, full_ph, chi_ph, pp_vertex, chi_pp, relabel):
    points, rows, order = gamma_ph.shape
    row_tiles, col_blocks = relabel.shape[1] // nblock, relabel.shape[2]
    high, wide = rows // row_tiles, order // col_blocks
    total = points * row_tiles * col_blocks
    capacity = -(-total // nboson) + 1
    bf16, f32 = jnp.bfloat16, jnp.float32
    chunks, cols = points * PARTS, order // PARTS
    whole = pltpu.VMEM((chunks, order, cols), bf16)
    blocks = pltpu.VMEM((chunks, rows, cols), bf16)
    shard = pltpu.VMEM(gamma_ph.shape, bf16)
    slabs = pltpu.VMEM((nboson, capacity, high, wide), bf16)
    table_rows = -(-(nboson * capacity) // LANES) * 8
    for count in (nboson, points, row_tiles * col_blocks, col_blocks, PARTS):
        assert count & (count - 1) == 0
    vmem = pl.BlockSpec(memory_space=pltpu.VMEM)
    hbm = pl.BlockSpec(memory_space=pl.ANY)
    smem = pl.BlockSpec(memory_space=pltpu.SMEM)
    operands = (relabel.transpose(1, 2, 0), gamma_ph, full_ph, chi_ph, pp_vertex, chi_pp)

    def window(lag):
        result = pltpu.VMEM(gamma_ph.shape, bf16)
        early = lag is not None
        return pl.pallas_call(
            functools.partial(kernel, nboson, nblock, row_tiles, col_blocks, lag),
            out_shape=(result, jax.ShapeDtypeStruct((1, 1), jnp.int32)) if early else result,
            name="early" if early else "plain",
            in_specs=[hbm, hbm, hbm, vmem, hbm, vmem], out_specs=(vmem, smem) if early else vmem,
            scratch_shapes=[
                whole, whole, blocks, blocks, shard, shard, pltpu.VMEM((chunks, rows, cols), f32),
                pltpu.VMEM((total, high, wide), bf16), slabs, slabs, slabs, slabs,
                pltpu.VMEM(operands[0].shape, jnp.int32),
                pltpu.VMEM((table_rows, LANES), jnp.int32), pltpu.SMEM((table_rows, LANES), jnp.int32),
                pltpu.VMEM((8, LANES), jnp.int32), pltpu.SMEM((8, LANES), jnp.int32),
                DMA, DMA((3,)), pltpu.SemaphoreType.REGULAR((bits(nboson),)), DMA((nboson,)), DMA((nboson,)), DMA((nboson,)), DMA((nboson,)),
            ] + gather_scratch(nblock, points) + gather_scratch(nblock, points),
            compiler_params=pltpu.CompilerParams(
                collective_id=int(early), has_side_effects=True, vmem_limit_bytes=60 * 1024 * 1024),
        )(*operands)

    if capacity <= chunks - LAG or nboson * nblock > LANES:
        return window(None)
    result, late = window(LAG)
    return lax.cond(late[0, 0] == 0, lambda: result, lambda: window(None))


def solution(mesh):
    placed = (
        P("boson", "block", None),
        P("boson", "block", None),
        P("boson", None),
        P("boson", "block", None),
        P("boson", None),
        P(),
    )
    return jax.shard_map(
        functools.partial(local, mesh.shape["boson"], mesh.shape["block"]), mesh=mesh,
        in_specs=placed, out_specs=P("boson", "block", None), check_vma=False,
    )
```

```python
import functools
import jax
import jax.numpy as jnp
from jax import lax
from jax.experimental import pallas as pl
from jax.experimental.pallas import tpu as pltpu
from jax.sharding import PartitionSpec as P

MESH = pl.DeviceIdType.MESH
DMA = pltpu.SemaphoreType.DMA
PARTS = 4
FIXED = 2
LAG = 2
LANES = 128


def loop(start, stop, body):
    lax.fori_loop(start, stop, lambda i, carry: (body(i), carry)[1], 0)


class Gather:
    def __init__(self, nblock, shard, blocks, whole, fixed, sems):
        self.nblock, self.shard, self.blocks, self.whole = nblock, shard, blocks, whole
        self.far_s, self.far_r, self.near_s, self.near_r, self.fwd_s, self.fwd_r, self.loc = sems
        self.chunks, _, self.cols = whole.shape
        self.rows = shard.shape[1]
        self.fixed = fixed
        self.boson = lax.axis_index("boson")
        self.here = lax.axis_index("block")
        self.partner = self.here + 1 - 2 * (self.here % 2)

    def peers(self):
        out = [self.partner]
        for j in range(1, self.nblock // 2):
            out.append((self.here + 2 * j) & (self.nblock - 1))
        return out

    def place(self, g, owner):
        rows = pl.ds(pl.multiple_of(owner * self.rows, self.rows), self.rows)
        return self.whole.at[g, rows]

    def load(self, g):
        source = self.shard.at[g // PARTS, :, g % PARTS * self.cols:(g % PARTS + 1) * self.cols]
        target = self.place(g, self.here) if g < self.fixed else self.blocks.at[g]
        return pltpu.make_async_copy(source, target, self.loc.at[g])

    def pack(self, order):
        def one(g):
            self.place(g, self.here)[...] = self.blocks[order(g)]
        loop(self.fixed, self.chunks, one)

    def far(self, g, j, owner):
        return pltpu.make_async_remote_copy(
            src_ref=self.place(g, owner), dst_ref=self.place(g, owner),
            send_sem=self.far_s.at[j - 1, g], recv_sem=self.far_r.at[j - 1, g],
            device_id=(self.boson, (self.here + 2 * j) & (self.nblock - 1)), device_id_type=MESH)

    def near(self, g, owner):
        return pltpu.make_async_remote_copy(
            src_ref=self.place(g, owner), dst_ref=self.place(g, owner),
            send_sem=self.near_s.at[g], recv_sem=self.near_r.at[g],
            device_id=(self.boson, self.partner), device_id_type=MESH)

    def forward(self, g, j, owner):
        return pltpu.make_async_remote_copy(
            src_ref=self.place(g, owner), dst_ref=self.place(g, owner),
            send_sem=self.fwd_s.at[j - 1, g], recv_sem=self.fwd_r.at[j - 1, g],
            device_id=(self.boson, self.partner), device_id_type=MESH)

    def each_far(self, act):
        for j in range(1, self.nblock // 2):
            act(j)

    def start_far(self, begin, end):
        loop(begin, end, lambda g: self.each_far(lambda j: self.far(g, j, self.here).start()))

    def start_near(self, begin, end):
        loop(begin, end, lambda g: self.near(g, self.here).start())

    def relay(self, g):
        def one(j):
            owner = (self.here + self.nblock - 2 * j) & (self.nblock - 1)
            self.far(g, j, owner).wait_recv()
            self.forward(g, j, owner).start()
        self.each_far(one)

    def arrived(self, g):
        self.near(g, self.partner).wait_recv()
        def one(j):
            twin = (self.partner + self.nblock - 2 * j) & (self.nblock - 1)
            self.forward(g, j, twin).wait_recv()
        self.each_far(one)

    def left(self, g):
        self.each_far(lambda j: self.far(g, j, self.here).wait_send())

    def sent(self, begin, end):
        loop(begin, end, self.left)
        def one(g):
            self.near(g, self.here).wait_send()
            def fwd(j):
                owner = (self.here + self.nblock - 2 * j) & (self.nblock - 1)
                self.forward(g, j, owner).wait_send()
            self.each_far(fwd)
        loop(0, self.chunks, one)


def gather_scratch(nblock, points):
    far, chunks = max(nblock // 2 - 1, 1), points * PARTS
    return [DMA((far, chunks)), DMA((far, chunks)), DMA((chunks,)), DMA((chunks,)),
            DMA((far, chunks)), DMA((far, chunks)), DMA((chunks,))]


class Exchange:
    def __init__(self, nboson, outgoing, incoming, send, recv):
        self.n, self.outgoing, self.incoming = nboson, outgoing, incoming
        self.send, self.recv = send, recv
        self.capacity = outgoing.shape[1]
        self.boson = lax.axis_index("boson")
        self.block = lax.axis_index("block")

    def shift(self, i):
        return self.n // 2 + (1 - 2 * (i & 1)) * ((i + 1) >> 1)

    def copy(self, s, slot, start=0, size=None):
        dest = (self.boson + s) & (self.n - 1)
        slots = pl.ds(start, self.capacity if size is None else size)
        return pltpu.make_async_remote_copy(
            src_ref=self.outgoing.at[dest, slots], dst_ref=self.incoming.at[slot, slots],
            send_sem=self.send.at[s], recv_sem=self.recv.at[s],
            device_id=(dest, self.block), device_id_type=MESH)

    def pack(self, target, dest, tiles, table, start, size):
        for k in range(size):
            target[dest, start + k] = tiles[table[dest * self.capacity + start + k]]

    def part(self, tiles, table, start, size, first=False, last=False):
        behind = (start if first else start - 1, size - first + last)
        def pack(i, slots):
            dest = (self.boson + self.shift(i)) & (self.n - 1)
            self.pack(self.outgoing, dest, tiles, table, *slots)
        def send(i, slots):
            self.copy(self.shift(i), self.boson, *slots).start()
        now = (start, size)
        pack(0, now)
        def one(i):
            pack(i, now)
            send(i - 1, now)
        loop(1, self.n - 3, one)
        waiting = functools.partial(send, self.n - 4, now)
        if behind[1] > 0:
            for i in (self.n - 3, self.n - 2):
                pack(i, behind)
                waiting()
                waiting = functools.partial(send, i, behind)
        return waiting

    def keep(self, tiles, table):
        self.pack(self.incoming, self.boson, tiles, table, 0, self.capacity)

    def received(self):
        loop(1, self.n, lambda s: self.copy(s, (self.boson + self.n - s) & (self.n - 1)).wait_recv())

    def sent(self):
        loop(1, self.n, lambda s: self.copy(s, self.boson).wait_send())


class Greeting:
    def __init__(self, nboson, block_peers, met):
        self.barrier, self.met = pltpu.get_barrier_semaphore(), met
        boson, block = lax.axis_index("boson"), lax.axis_index("block")
        self.pairs = [(boson + (1 - 2 * (boson // 2 ** bit % 2)) * 2 ** bit, block)
                      for bit in range(bits(nboson))]
        self.peers = [(boson, peer) for peer in block_peers] + self.pairs

    def say(self):
        for peer in self.peers:
            pl.semaphore_signal(self.barrier, inc=1, device_id=peer, device_id_type=MESH)

    def hear(self):
        pl.semaphore_wait(self.barrier, len(self.peers))

    def tell(self, bit):
        pl.semaphore_signal(self.met.at[bit], inc=1, device_id=self.pairs[bit], device_id_type=MESH)

    def pass_on(self, bit):
        pl.semaphore_wait(self.met.at[bit], 1)
        if bit + 1 < len(self.pairs):
            self.tell(bit + 1)


class Plan:
    def __init__(self, *runs):
        self.runs = runs

    def due(self):
        chunk = slot = 0
        for times, chunks, slots in self.runs:
            for _ in range(times):
                chunk, slot = chunk + chunks, slot + slots
                yield chunk, slot


def plans(chunks, lag):
    ahead = Plan((1, lag + 1, 1), (chunks - lag - 1, 1, 1))
    return ahead, Plan((1, lag + 1, 1), ((chunks - lag - 2) // 2, 2, 2))


def bits(count):
    return count.bit_length() - 1


class Items:
    def __init__(self, nboson, targets, first_row, row_tiles, boson=None):
        _, col_blocks, count = targets.shape
        points, per_point = count // nboson, row_tiles * col_blocks
        self.total, self.chunks, self.pair = points * per_point, points * PARTS, col_blocks // PARTS
        self.row_tiles = row_tiles
        flat = targets[pl.ds(first_row, row_tiles)].reshape(per_point, count)
        lane = lax.broadcasted_iota(jnp.int32, flat.shape, 1)
        own = jnp.concatenate(
            [flat[:, q:q + 1] if boson is None else
             jnp.sum(jnp.where(lane == boson * points + q, flat, 0), axis=1, keepdims=True)
             for q in range(points)], axis=0)
        self.item = lax.broadcasted_iota(jnp.int32, (self.total, 1), 0)
        self.shift = ((own >> bits(points)) - (0 if boson is None else boson)) & (nboson - 1)
        self.row = (self.item >> bits(col_blocks)) & (row_tiles - 1)
        self.column = self.item & (col_blocks - 1)
        self.target = (own & (points - 1)) * per_point + (self.item & (per_point - 1))
        part = self.column >> bits(self.pair)
        self.ahead = (self.item >> bits(per_point)) * PARTS + part
        self.home = (own & (points - 1)) * PARTS + part

    def spread(self, keys, values, width):
        wanted = lax.broadcasted_iota(jnp.int32, (self.total, width), 1)
        return jnp.sum(jnp.where(keys == wanted, values, 0), axis=0, keepdims=True)

    def tile(self, chunk, places):
        if places is not None:
            lane = lax.broadcasted_iota(jnp.int32, (self.total, places.shape[1]), 1)
            chunk = jnp.sum(jnp.where(chunk == lane, places, 0), axis=1, keepdims=True)
        return (chunk * self.row_tiles + self.row) * self.pair + (self.column & (self.pair - 1))


def slot_tables(nboson, capacity, items, ahead_places, home_places, rows):
    boson = lax.axis_index("boson")
    same = items.spread(items.item, items.shift, items.total) == items.shift
    def rank(key):
        later = same & (items.spread(items.item, key, items.total) > key)
        return capacity - 1 - jnp.sum(jnp.where(later, 1, 0), axis=1, keepdims=True)

    there = ((boson + items.shift) & (nboson - 1)) * capacity
    here = ((boson - items.shift) & (nboson - 1)) * capacity
    ahead = items.tile(items.ahead, ahead_places)
    home = items.tile(items.home, home_places)
    out_rank, back_rank = rank(ahead), rank(home)
    width = rows.shape[0] // 8 * rows.shape[1]
    last_slot, last_item = nboson * capacity - 1, items.total - 1
    for k, (keys, values, last) in enumerate((
            (items.item, there + back_rank, last_slot), (there + out_rank, ahead, last_item),
            (items.target, here + out_rank, last_slot), (here + back_rank, home, last_item))):
        line = jnp.clip(items.spread(keys, values, width), 0, last)
        for h in range(width // LANES):
            rows[h * 8 + k:h * 8 + k + 1, :] = line[:, h * LANES:(h + 1) * LANES]


def choose_orders(nboson, nblock, capacity, fixed, plans, targets, row_tiles, rows):
    def counts(pick, items_of):
        total = 0.
        for b, items in enumerate(items_of):
            lane = lax.broadcasted_iota(jnp.int32, (items.total, LANES), 1)
            hot = jnp.where(lane == b * nboson + items.shift, 1., 0.).astype(jnp.bfloat16)
            chunk = items.spread(items.item, pick(items), items.total)
            turn = lax.broadcasted_iota(jnp.int32, (items.chunks, items.total), 0)
            member = jnp.where(chunk == turn, 1., 0.).astype(jnp.bfloat16)
            total = total + jnp.dot(member, hot, preferred_element_type=jnp.float32)
        return total

    items_of = [Items(nboson, targets, b * row_tiles, row_tiles) for b in range(nblock)]
    chunks = items_of[0].chunks
    lane = lax.broadcasted_iota(jnp.int32, (1, LANES), 1)
    weighed = (lane < nboson * nblock) & ((lane & (nboson - 1)) > 0)
    chunk = lax.broadcasted_iota(jnp.int32, (chunks, 1), 0)
    shift = lane & (nboson - 1)
    behind = jnp.where((shift == 1) | (shift == nboson - 1), 1., 0.)
    tables, begin = [], []
    for pick, held in zip((lambda i: i.ahead, lambda i: i.home), fixed):
        count = counts(pick, items_of)
        gain = jnp.exp(-2. * jnp.minimum(count, 30.))
        spare = capacity - jnp.sum(count, axis=0, keepdims=True) + behind
        ready = spare + jnp.sum(jnp.where(chunk < held, count, 0.), axis=0, keepdims=True)
        tables.append((count, gain, spare))
        begin.append((jnp.where(weighed, jnp.exp(-2. * jnp.clip(ready, -30., 30.)), 0.),
                      jnp.broadcast_to(jnp.where(chunk < held, chunk, -1), (chunks, LANES))))

    def choose(t, state, held=(0, 0)):
        out = []
        for (weight, turn), (_, gain, _), first in zip(state, tables, held):
            if isinstance(t, int) and t < first:
                out.append((weight, turn))
                continue
            score = jnp.sum(weight * gain, axis=1, keepdims=True)
            score = jnp.where(turn < 0, score, jnp.inf)
            best = jnp.min(score, axis=0, keepdims=True)
            index = lax.broadcasted_iota(jnp.int32, score.shape, 0)
            hit = index == jnp.min(jnp.where(score == best, index, chunks), axis=0, keepdims=True)
            weight = weight * jnp.sum(jnp.where(hit, gain, 0.), axis=0, keepdims=True)
            out.append((weight, jnp.where(hit, t, turn)))
        return tuple(out)

    state = tuple(begin)
    for held in range(min(fixed), max(fixed)):
        state = choose(held, state, fixed)
    chosen = lax.fori_loop(max(fixed), chunks, choose, state)
    late = jnp.zeros((1, LANES), jnp.float32)
    turns = []
    for k, ((_, turn), (count, _, spare), plan) in enumerate(zip(chosen, tables, plans)):
        index = lax.broadcasted_iota(jnp.int32, turn.shape, 0)
        column = lax.broadcasted_iota(jnp.int32, turn.shape, 1)
        order = jnp.sum(jnp.where(turn == column, index, 0), axis=0, keepdims=True)
        rows[k:k + 1, :] = jnp.clip(order, 0, chunks - 1)
        turned = jnp.sum(jnp.where(index == column, turn, 0), axis=0, keepdims=True)
        turns.append(jnp.clip(turned, 0, chunks - 1))
        rows[k + 2:k + 3, :] = turns[k]
        for done, slots in plan.due():
            ready = jnp.sum(jnp.where(turn < done, count, 0.), axis=0, keepdims=True)
            late = late + jnp.where(weighed & (ready + spare < slots), 1., 0.)
    return turns, jnp.sum(late, axis=1, keepdims=True)


class Table:
    def __init__(self, ref, k, size):
        self.ref, self.k, self.size = ref, k, size

    def __getitem__(self, i):
        if self.size <= LANES:
            return self.ref[self.k, i]
        return self.ref[(i >> bits(LANES)) * 8 + self.k, i & (LANES - 1)]


def kernel(nboson, nblock, row_tiles, col_blocks, lag, *refs):
    relabel, gamma_in, full_in, chi_ph, pp_in, chi_pp, out, *refs = refs
    early = lag is not None
    late, refs = (refs[0], refs[1:]) if early else (None, refs)
    (full, pp, full_blocks, pp_blocks, gamma, scaled, base, sums, tiles, packed, landed, back, returned,
     targets, table_rows, table, order_rows, orders,
     gamma_sem, table_sem, met, ahead_s, ahead_r, home_s, home_r, *gather_sems) = refs
    half = len(gather_sems) // 2
    chunks = full.shape[0]
    fixed, free = (FIXED, 0) if early else (chunks, chunks)
    first = Gather(nblock, full_in, full_blocks, full, fixed, gather_sems[:half])
    second = Gather(nblock, pp_in, pp_blocks, pp, free, gather_sems[half:])
    ahead_plan, home_plan = plans(chunks, lag) if early else (Plan(), Plan())
    ahead = Exchange(nboson, packed, landed, ahead_s, ahead_r)
    home = Exchange(nboson, back, returned, home_s, home_r)
    points, rows, order = gamma.shape
    high, wide = rows // row_tiles, order // col_blocks
    pair = first.cols // wide
    capacity = landed.shape[1]
    items_here, slots = points * row_tiles * col_blocks, nboson * capacity
    send_slot, item_of, back_slot, back_item_of = (
        Table(table, k, size) for k, size in enumerate((items_here, slots, items_here, slots)))
    load_targets = pltpu.make_async_copy(relabel, targets, table_sem.at[0])
    load_table = pltpu.make_async_copy(table_rows, table, table_sem.at[1])
    load_gamma = pltpu.make_async_copy(gamma_in, gamma, gamma_sem)

    greeting = Greeting(nboson, first.peers(), met)
    greeting.say()
    load_targets.start()
    for g in range(fixed):
        first.load(g).start()
    greeting.hear()
    for g in range(fixed):
        first.load(g).wait()
    first.start_far(0, fixed)
    greeting.tell(0)
    for g in range(fixed, chunks):
        first.load(g).start()
    first.start_near(0, fixed)
    load_gamma.start()
    load_targets.wait()
    if early:
        turns, count = choose_orders(
            nboson, nblock, capacity, (fixed, free), (ahead_plan, home_plan), targets, row_tiles,
            order_rows)
        load_orders = pltpu.make_async_copy(order_rows, orders, table_sem.at[2])
        load_orders.start()
        late[0, 0] = jnp.where(jnp.sum(count) > 0, 1, 0)
        for g in range(fixed, chunks):
            first.load(g).wait()
        load_orders.wait()
        first.pack(lambda g: orders[0, g])
        first.start_far(fixed, chunks)
    else:
        turns = None, None

    items = Items(nboson, targets, lax.axis_index("block") * row_tiles, row_tiles,
                  lax.axis_index("boson"))
    slot_tables(nboson, capacity, items, *turns, table_rows)
    if early:
        first.start_near(fixed, chunks)
    load_table.start()
    for bit in range(bits(nboson)):
        greeting.pass_on(bit)
    first.relay(0)
    load_gamma.wait()
    for q in range(points):
        scaled[q] = (gamma[q].astype(jnp.float32) * chi_ph[q:q + 1, :]).astype(jnp.bfloat16)
    load_table.wait()
    for g in range(chunks):
        second.load(g).start()
    first.relay(1)

    def product(gather, g, k):
        point = (orders[k, g] if early else g) >> bits(PARTS)
        phi = jnp.dot(scaled[point], gather.whole[g], preferred_element_type=jnp.float32)
        wire = phi.astype(jnp.bfloat16)
        for r in range(row_tiles):
            for i in range(pair):
                tiles[(g * row_tiles + r) * pair + i] = (
                    wire[r * high:(r + 1) * high, i * wide:(i + 1) * wide])
        return phi

    def staged(exchange, table, plan, step):
        chunk = slot = 0
        for times, span, slots in plan.runs:
            def one(i, chunk=chunk, slot=slot, span=span, slots=slots):
                begin = chunk + i * span
                loop(begin, begin + span, step)
                exchange.part(tiles, table, slot + i * slots, slots, first=slot == 0)()
            one(0) if times == 1 else loop(0, times, one)
            chunk, slot = chunk + times * span, slot + times * slots
        loop(chunk, chunks, step)
        last = exchange.part(tiles, table, slot, capacity - slot, first=slot == 0, last=True)
        exchange.keep(tiles, table)
        last()

    def ahead_step(g):
        @pl.when(g == chunks - 3)
        def _():
            for i in range(chunks):
                second.load(i).wait()
            if early:
                second.pack(lambda i: orders[1, i])
        @pl.when(g == chunks - 1)
        def _():
            first.left(chunks - 1)
            second.start_far(0, chunks)
        @pl.when(g > 1)
        def _():
            first.relay(g)
        first.arrived(g)
        base[g] = product(first, g, 0)

    staged(ahead, item_of, ahead_plan, ahead_step)
    second.start_near(0, chunks)
    first.sent(0, chunks - 1)
    waiting = chunks // 4
    loop(0, waiting, second.relay)
    ahead.received()

    flat = landed.reshape(nboson * capacity, high, wide)
    def unpack(p):
        chi = chi_pp[pl.ds(p, 1), :]
        for c in range(col_blocks):
            for r in range(row_tiles):
                tile = flat[back_slot[(p * row_tiles + r) * col_blocks + c]]
                scaled[p, r * high:(r + 1) * high, c * wide:(c + 1) * wide] = (
                    tile.astype(jnp.float32) * chi[:, c * wide:(c + 1) * wide]).astype(jnp.bfloat16)
    loop(0, points, unpack)

    def home_step(g):
        @pl.when(g >= waiting)
        def _():
            second.relay(g)
        second.arrived(g)
        product(second, g, 1)

    staged(home, back_item_of, home_plan, home_step)
    def settle(q):
        for part in range(PARTS):
            chunk = q * PARTS + part
            at = (q, slice(None), slice(part * first.cols, (part + 1) * first.cols))
            sums[at] = gamma[at].astype(jnp.float32) + base[orders[2, chunk] if early else chunk]
    loop(0, points, settle)
    ahead.sent()
    second.sent(0, chunks)
    home.received()

    flat_back = returned.reshape(nboson * capacity, high, wide)
    def finish(q):
        for c in range(col_blocks):
            for r in range(row_tiles):
                tile = flat_back[send_slot[(q * row_tiles + r) * col_blocks + c]]
                at = (q, slice(r * high, (r + 1) * high), slice(c * wide, (c + 1) * wide))
                out[at] = (sums[at] + tile.astype(jnp.float32)).astype(jnp.bfloat16)
    loop(0, points, finish)
    home.sent()


def local(nboson, nblock, gamma_ph, full_ph, chi_ph, pp_vertex, chi_pp, relabel):
    points, rows, order = gamma_ph.shape
    row_tiles, col_blocks = relabel.shape[1] // nblock, relabel.shape[2]
    high, wide = rows // row_tiles, order // col_blocks
    total = points * row_tiles * col_blocks
    capacity = -(-total // nboson) + 1
    bf16, f32 = jnp.bfloat16, jnp.float32
    chunks, cols = points * PARTS, order // PARTS
    whole = pltpu.VMEM((chunks, order, cols), bf16)
    blocks = pltpu.VMEM((chunks, rows, cols), bf16)
    shard = pltpu.VMEM(gamma_ph.shape, bf16)
    slabs = pltpu.VMEM((nboson, capacity, high, wide), bf16)
    table_rows = -(-(nboson * capacity) // LANES) * 8
    for count in (nboson, nblock, points, row_tiles * col_blocks, col_blocks, PARTS):
        assert count & (count - 1) == 0
    vmem = pl.BlockSpec(memory_space=pltpu.VMEM)
    hbm = pl.BlockSpec(memory_space=pl.ANY)
    smem = pl.BlockSpec(memory_space=pltpu.SMEM)
    operands = (relabel.transpose(1, 2, 0), gamma_ph, full_ph, chi_ph, pp_vertex, chi_pp)

    def window(lag):
        result = pltpu.VMEM(gamma_ph.shape, bf16)
        early = lag is not None
        return pl.pallas_call(
            functools.partial(kernel, nboson, nblock, row_tiles, col_blocks, lag),
            out_shape=(result, jax.ShapeDtypeStruct((1, 1), jnp.int32)) if early else result,
            name="early" if early else "plain",
            in_specs=[hbm, hbm, hbm, vmem, hbm, vmem], out_specs=(vmem, smem) if early else vmem,
            scratch_shapes=[
                whole, whole, blocks, blocks, shard, shard, pltpu.VMEM((chunks, rows, cols), f32),
                pltpu.VMEM(gamma_ph.shape, f32),
                pltpu.VMEM((total, high, wide), bf16), slabs, slabs, slabs, slabs,
                pltpu.VMEM(operands[0].shape, jnp.int32),
                pltpu.VMEM((table_rows, LANES), jnp.int32), pltpu.SMEM((table_rows, LANES), jnp.int32),
                pltpu.VMEM((8, LANES), jnp.int32), pltpu.SMEM((8, LANES), jnp.int32),
                DMA, DMA((3,)), pltpu.SemaphoreType.REGULAR((bits(nboson),)), DMA((nboson,)), DMA((nboson,)), DMA((nboson,)), DMA((nboson,)),
            ] + gather_scratch(nblock, points) + gather_scratch(nblock, points),
            compiler_params=pltpu.CompilerParams(
                collective_id=int(early), has_side_effects=True, vmem_limit_bytes=60 * 1024 * 1024),
        )(*operands)

    if capacity <= chunks - LAG or nboson * nblock > LANES:
        return window(None)
    result, late = window(LAG)
    return lax.cond(late[0, 0] == 0, lambda: result, lambda: window(None))


def solution(mesh):
    placed = (
        P("boson", "block", None),
        P("boson", "block", None),
        P("boson", None),
        P("boson", "block", None),
        P("boson", None),
        P(),
    )
    return jax.shard_map(
        functools.partial(local, mesh.shape["boson"], mesh.shape["block"]), mesh=mesh,
        in_specs=placed, out_specs=P("boson", "block", None), check_vma=False,
    )
```

```python
import functools
import jax
import jax.numpy as jnp
from jax import lax
from jax.experimental import pallas as pl
from jax.experimental.pallas import tpu as pltpu
from jax.sharding import PartitionSpec as P

MESH = pl.DeviceIdType.MESH
DMA = pltpu.SemaphoreType.DMA
PARTS = 4
FIXED = 2
LAG = 2
LANES = 128


def loop(start, stop, body):
    lax.fori_loop(start, stop, lambda i, carry: (body(i), carry)[1], 0)


class Gather:
    def __init__(self, nblock, shard, blocks, whole, fixed, sems):
        self.nblock, self.shard, self.blocks, self.whole = nblock, shard, blocks, whole
        self.far_s, self.far_r, self.near_s, self.near_r, self.fwd_s, self.fwd_r, self.loc = sems
        self.chunks, _, self.cols = whole.shape
        self.rows = shard.shape[1]
        self.fixed = fixed
        self.boson = lax.axis_index("boson")
        self.here = lax.axis_index("block")
        self.partner = self.here + 1 - 2 * (self.here % 2)

    def peers(self):
        out = [self.partner]
        for j in range(1, self.nblock // 2):
            out.append((self.here + 2 * j) & (self.nblock - 1))
        return out

    def place(self, g, owner):
        rows = pl.ds(pl.multiple_of(owner * self.rows, self.rows), self.rows)
        return self.whole.at[g, rows]

    def load(self, g):
        source = self.shard.at[g // PARTS, :, g % PARTS * self.cols:(g % PARTS + 1) * self.cols]
        target = self.place(g, self.here) if g < self.fixed else self.blocks.at[g]
        return pltpu.make_async_copy(source, target, self.loc.at[g])

    def pack(self, order):
        def one(g):
            self.place(g, self.here)[...] = self.blocks[order(g)]
        loop(self.fixed, self.chunks, one)

    def far(self, g, j, owner):
        return pltpu.make_async_remote_copy(
            src_ref=self.place(g, owner), dst_ref=self.place(g, owner),
            send_sem=self.far_s.at[j - 1, g], recv_sem=self.far_r.at[j - 1, g],
            device_id=(self.boson, (self.here + 2 * j) & (self.nblock - 1)), device_id_type=MESH)

    def near(self, g, owner):
        return pltpu.make_async_remote_copy(
            src_ref=self.place(g, owner), dst_ref=self.place(g, owner),
            send_sem=self.near_s.at[g], recv_sem=self.near_r.at[g],
            device_id=(self.boson, self.partner), device_id_type=MESH)

    def forward(self, g, j, owner):
        return pltpu.make_async_remote_copy(
            src_ref=self.place(g, owner), dst_ref=self.place(g, owner),
            send_sem=self.fwd_s.at[j - 1, g], recv_sem=self.fwd_r.at[j - 1, g],
            device_id=(self.boson, self.partner), device_id_type=MESH)

    def each_far(self, act):
        for j in range(1, self.nblock // 2):
            act(j)

    def start_far(self, begin, end):
        loop(begin, end, lambda g: self.each_far(lambda j: self.far(g, j, self.here).start()))

    def start_near(self, begin, end):
        loop(begin, end, lambda g: self.near(g, self.here).start())

    def relay(self, g):
        def one(j):
            owner = (self.here + self.nblock - 2 * j) & (self.nblock - 1)
            self.far(g, j, owner).wait_recv()
            self.forward(g, j, owner).start()
        self.each_far(one)

    def arrived(self, g):
        self.near(g, self.partner).wait_recv()
        def one(j):
            twin = (self.partner + self.nblock - 2 * j) & (self.nblock - 1)
            self.forward(g, j, twin).wait_recv()
        self.each_far(one)

    def left(self, g):
        self.each_far(lambda j: self.far(g, j, self.here).wait_send())

    def sent(self, begin, end):
        loop(begin, end, self.left)
        def one(g):
            self.near(g, self.here).wait_send()
            def fwd(j):
                owner = (self.here + self.nblock - 2 * j) & (self.nblock - 1)
                self.forward(g, j, owner).wait_send()
            self.each_far(fwd)
        loop(0, self.chunks, one)


def gather_scratch(nblock, points):
    far, chunks = max(nblock // 2 - 1, 1), points * PARTS
    return [DMA((far, chunks)), DMA((far, chunks)), DMA((chunks,)), DMA((chunks,)),
            DMA((far, chunks)), DMA((far, chunks)), DMA((chunks,))]


class Exchange:
    def __init__(self, nboson, outgoing, incoming, send, recv):
        self.n, self.outgoing, self.incoming = nboson, outgoing, incoming
        self.send, self.recv = send, recv
        self.capacity = outgoing.shape[1]
        self.boson = lax.axis_index("boson")
        self.block = lax.axis_index("block")

    def shift(self, i):
        return self.n // 2 + (1 - 2 * (i & 1)) * ((i + 1) >> 1)

    def copy(self, s, slot, start=0, size=None):
        dest = (self.boson + s) & (self.n - 1)
        slots = pl.ds(start, self.capacity if size is None else size)
        return pltpu.make_async_remote_copy(
            src_ref=self.outgoing.at[dest, slots], dst_ref=self.incoming.at[slot, slots],
            send_sem=self.send.at[s], recv_sem=self.recv.at[s],
            device_id=(dest, self.block), device_id_type=MESH)

    def pack(self, target, dest, tiles, table, start, size):
        for k in range(size):
            target[dest, start + k] = tiles[table[dest * self.capacity + start + k]]

    def part(self, tiles, table, start, size, first=False, last=False):
        behind = (start if first else start - 1, size - first + last)
        def pack(i, slots):
            dest = (self.boson + self.shift(i)) & (self.n - 1)
            self.pack(self.outgoing, dest, tiles, table, *slots)
        def send(i, slots):
            self.copy(self.shift(i), self.boson, *slots).start()
        now = (start, size)
        pack(0, now)
        def one(i):
            pack(i, now)
            send(i - 1, now)
        if first and last:
            loop(1, self.n - 3, one)
        else:
            for i in range(1, self.n - 3):
                one(i)
        waiting = functools.partial(send, self.n - 4, now)
        if behind[1] > 0:
            for i in (self.n - 3, self.n - 2):
                pack(i, behind)
                waiting()
                waiting = functools.partial(send, i, behind)
        return waiting

    def keep(self, tiles, table):
        self.pack(self.incoming, self.boson, tiles, table, 0, self.capacity)

    def received(self):
        loop(1, self.n, lambda s: self.copy(s, (self.boson + self.n - s) & (self.n - 1)).wait_recv())

    def sent(self):
        loop(1, self.n, lambda s: self.copy(s, self.boson).wait_send())


class Greeting:
    def __init__(self, nboson, block_peers, met):
        self.barrier, self.met = pltpu.get_barrier_semaphore(), met
        boson, block = lax.axis_index("boson"), lax.axis_index("block")
        self.pairs = [(boson + (1 - 2 * (boson // 2 ** bit % 2)) * 2 ** bit, block)
                      for bit in range(bits(nboson))]
        self.peers = [(boson, peer) for peer in block_peers] + self.pairs

    def say(self):
        for peer in self.peers:
            pl.semaphore_signal(self.barrier, inc=1, device_id=peer, device_id_type=MESH)

    def hear(self):
        pl.semaphore_wait(self.barrier, len(self.peers))

    def tell(self, bit):
        pl.semaphore_signal(self.met.at[bit], inc=1, device_id=self.pairs[bit], device_id_type=MESH)

    def pass_on(self, bit):
        pl.semaphore_wait(self.met.at[bit], 1)
        if bit + 1 < len(self.pairs):
            self.tell(bit + 1)


class Plan:
    def __init__(self, *runs):
        self.runs = runs

    def due(self):
        chunk = slot = 0
        for times, chunks, slots in self.runs:
            for _ in range(times):
                chunk, slot = chunk + chunks, slot + slots
                yield chunk, slot


def plans(chunks, lag):
    ahead = Plan((1, lag + 1, 1), (chunks - lag - 1, 1, 1))
    return ahead, Plan((1, lag + 1, 1), ((chunks - lag - 2) // 2, 2, 2))


def bits(count):
    return count.bit_length() - 1


class Items:
    def __init__(self, nboson, targets, first_row, row_tiles, boson=None):
        _, col_blocks, count = targets.shape
        points, per_point = count // nboson, row_tiles * col_blocks
        self.total, self.chunks, self.pair = points * per_point, points * PARTS, col_blocks // PARTS
        self.row_tiles = row_tiles
        flat = targets[pl.ds(first_row, row_tiles)].reshape(per_point, count)
        lane = lax.broadcasted_iota(jnp.int32, flat.shape, 1)
        own = jnp.concatenate(
            [flat[:, q:q + 1] if boson is None else
             jnp.sum(jnp.where(lane == boson * points + q, flat, 0), axis=1, keepdims=True)
             for q in range(points)], axis=0)
        self.item = lax.broadcasted_iota(jnp.int32, (self.total, 1), 0)
        self.shift = ((own >> bits(points)) - (0 if boson is None else boson)) & (nboson - 1)
        self.row = (self.item >> bits(col_blocks)) & (row_tiles - 1)
        self.column = self.item & (col_blocks - 1)
        self.target = (own & (points - 1)) * per_point + (self.item & (per_point - 1))
        part = self.column >> bits(self.pair)
        self.ahead = (self.item >> bits(per_point)) * PARTS + part
        self.home = (own & (points - 1)) * PARTS + part

    def spread(self, keys, values, width):
        wanted = lax.broadcasted_iota(jnp.int32, (self.total, width), 1)
        return jnp.sum(jnp.where(keys == wanted, values, 0), axis=0, keepdims=True)

    def tile(self, chunk, places):
        if places is not None:
            lane = lax.broadcasted_iota(jnp.int32, (self.total, places.shape[1]), 1)
            chunk = jnp.sum(jnp.where(chunk == lane, places, 0), axis=1, keepdims=True)
        return (chunk * self.row_tiles + self.row) * self.pair + (self.column & (self.pair - 1))


def slot_tables(nboson, capacity, items, ahead_places, home_places, rows):
    boson = lax.axis_index("boson")
    same = items.spread(items.item, items.shift, items.total) == items.shift
    def rank(key):
        later = same & (items.spread(items.item, key, items.total) > key)
        return capacity - 1 - jnp.sum(jnp.where(later, 1, 0), axis=1, keepdims=True)

    there = ((boson + items.shift) & (nboson - 1)) * capacity
    here = ((boson - items.shift) & (nboson - 1)) * capacity
    ahead = items.tile(items.ahead, ahead_places)
    home = items.tile(items.home, home_places)
    out_rank, back_rank = rank(ahead), rank(home)
    width = rows.shape[0] // 8 * rows.shape[1]
    last_slot, last_item = nboson * capacity - 1, items.total - 1
    for k, (keys, values, last) in enumerate((
            (items.item, there + back_rank, last_slot), (there + out_rank, ahead, last_item),
            (items.target, here + out_rank, last_slot), (here + back_rank, home, last_item))):
        line = jnp.clip(items.spread(keys, values, width), 0, last)
        for h in range(width // LANES):
            rows[h * 8 + k:h * 8 + k + 1, :] = line[:, h * LANES:(h + 1) * LANES]


def choose_orders(nboson, nblock, capacity, fixed, plans, targets, row_tiles, rows):
    def counts(pick, items_of):
        total = 0.
        for b, items in enumerate(items_of):
            lane = lax.broadcasted_iota(jnp.int32, (items.total, LANES), 1)
            hot = jnp.where(lane == b * nboson + items.shift, 1., 0.).astype(jnp.bfloat16)
            chunk = items.spread(items.item, pick(items), items.total)
            turn = lax.broadcasted_iota(jnp.int32, (items.chunks, items.total), 0)
            member = jnp.where(chunk == turn, 1., 0.).astype(jnp.bfloat16)
            total = total + jnp.dot(member, hot, preferred_element_type=jnp.float32)
        return total

    items_of = [Items(nboson, targets, b * row_tiles, row_tiles) for b in range(nblock)]
    chunks = items_of[0].chunks
    lane = lax.broadcasted_iota(jnp.int32, (1, LANES), 1)
    weighed = (lane < nboson * nblock) & ((lane & (nboson - 1)) > 0)
    chunk = lax.broadcasted_iota(jnp.int32, (chunks, 1), 0)
    shift = lane & (nboson - 1)
    behind = jnp.where((shift == 1) | (shift == nboson - 1), 1., 0.)
    tables, begin = [], []
    for pick, held in zip((lambda i: i.ahead, lambda i: i.home), fixed):
        count = counts(pick, items_of)
        gain = jnp.exp(-2. * jnp.minimum(count, 30.))
        spare = capacity - jnp.sum(count, axis=0, keepdims=True) + behind
        ready = spare + jnp.sum(jnp.where(chunk < held, count, 0.), axis=0, keepdims=True)
        tables.append((count, gain, spare))
        begin.append((jnp.where(weighed, jnp.exp(-2. * jnp.clip(ready, -30., 30.)), 0.),
                      jnp.broadcast_to(jnp.where(chunk < held, chunk, -1), (chunks, LANES))))

    def choose(t, state, held=(0, 0)):
        out = []
        for (weight, turn), (_, gain, _), first in zip(state, tables, held):
            if isinstance(t, int) and t < first:
                out.append((weight, turn))
                continue
            score = jnp.sum(weight * gain, axis=1, keepdims=True)
            score = jnp.where(turn < 0, score, jnp.inf)
            best = jnp.min(score, axis=0, keepdims=True)
            index = lax.broadcasted_iota(jnp.int32, score.shape, 0)
            hit = index == jnp.min(jnp.where(score == best, index, chunks), axis=0, keepdims=True)
            weight = weight * jnp.sum(jnp.where(hit, gain, 0.), axis=0, keepdims=True)
            out.append((weight, jnp.where(hit, t, turn)))
        return tuple(out)

    state = tuple(begin)
    for held in range(min(fixed), max(fixed)):
        state = choose(held, state, fixed)
    chosen = lax.fori_loop(max(fixed), chunks, choose, state)
    late = jnp.zeros((1, LANES), jnp.float32)
    turns = []
    for k, ((_, turn), (count, _, spare), plan) in enumerate(zip(chosen, tables, plans)):
        index = lax.broadcasted_iota(jnp.int32, turn.shape, 0)
        column = lax.broadcasted_iota(jnp.int32, turn.shape, 1)
        order = jnp.sum(jnp.where(turn == column, index, 0), axis=0, keepdims=True)
        rows[k:k + 1, :] = jnp.clip(order, 0, chunks - 1)
        turned = jnp.sum(jnp.where(index == column, turn, 0), axis=0, keepdims=True)
        turns.append(jnp.clip(turned, 0, chunks - 1))
        rows[k + 2:k + 3, :] = turns[k]
        for done, slots in plan.due():
            ready = jnp.sum(jnp.where(turn < done, count, 0.), axis=0, keepdims=True)
            late = late + jnp.where(weighed & (ready + spare < slots), 1., 0.)
    return turns, jnp.sum(late, axis=1, keepdims=True)


class Table:
    def __init__(self, ref, k, size):
        self.ref, self.k, self.size = ref, k, size

    def __getitem__(self, i):
        if self.size <= LANES:
            return self.ref[self.k, i]
        return self.ref[(i >> bits(LANES)) * 8 + self.k, i & (LANES - 1)]


def kernel(nboson, nblock, row_tiles, col_blocks, lag, *refs):
    relabel, gamma_in, full_in, chi_ph, pp_in, chi_pp, out, *refs = refs
    early = lag is not None
    late, refs = (refs[0], refs[1:]) if early else (None, refs)
    (full, pp, full_blocks, pp_blocks, gamma, scaled, base, sums, tiles, packed, landed, back, returned,
     targets, table_rows, table, order_rows, orders,
     gamma_sem, table_sem, met, ahead_s, ahead_r, home_s, home_r, *gather_sems) = refs
    half = len(gather_sems) // 2
    chunks = full.shape[0]
    fixed, free = (FIXED, 0) if early else (chunks, chunks)
    first = Gather(nblock, full_in, full_blocks, full, fixed, gather_sems[:half])
    second = Gather(nblock, pp_in, pp_blocks, pp, free, gather_sems[half:])
    ahead_plan, home_plan = plans(chunks, lag) if early else (Plan(), Plan())
    ahead = Exchange(nboson, packed, landed, ahead_s, ahead_r)
    home = Exchange(nboson, back, returned, home_s, home_r)
    points, rows, order = gamma.shape
    high, wide = rows // row_tiles, order // col_blocks
    pair = first.cols // wide
    capacity = landed.shape[1]
    items_here, slots = points * row_tiles * col_blocks, nboson * capacity
    send_slot, item_of, back_slot, back_item_of = (
        Table(table, k, size) for k, size in enumerate((items_here, slots, items_here, slots)))
    load_targets = pltpu.make_async_copy(relabel, targets, table_sem.at[0])
    load_table = pltpu.make_async_copy(table_rows, table, table_sem.at[1])
    load_gamma = pltpu.make_async_copy(gamma_in, gamma, gamma_sem)

    greeting = Greeting(nboson, first.peers(), met)
    greeting.say()
    load_targets.start()
    for g in range(fixed):
        first.load(g).start()
    greeting.hear()
    for g in range(fixed):
        first.load(g).wait()
    first.start_far(0, fixed)
    greeting.tell(0)
    for g in range(fixed, chunks):
        first.load(g).start()
    first.start_near(0, fixed)
    load_gamma.start()
    load_targets.wait()
    if early:
        turns, count = choose_orders(
            nboson, nblock, capacity, (fixed, free), (ahead_plan, home_plan), targets, row_tiles,
            order_rows)
        load_orders = pltpu.make_async_copy(order_rows, orders, table_sem.at[2])
        load_orders.start()
        late[0, 0] = jnp.where(jnp.sum(count) > 0, 1, 0)
        for g in range(fixed, chunks):
            first.load(g).wait()
        load_orders.wait()
        first.pack(lambda g: orders[0, g])
        first.start_far(fixed, chunks)
    else:
        turns = None, None

    items = Items(nboson, targets, lax.axis_index("block") * row_tiles, row_tiles,
                  lax.axis_index("boson"))
    slot_tables(nboson, capacity, items, *turns, table_rows)
    if early:
        first.start_near(fixed, chunks)
    load_table.start()
    for bit in range(bits(nboson)):
        greeting.pass_on(bit)
    first.relay(0)
    load_gamma.wait()
    for q in range(points):
        scaled[q] = (gamma[q].astype(jnp.float32) * chi_ph[q:q + 1, :]).astype(jnp.bfloat16)
    load_table.wait()
    for g in range(chunks):
        second.load(g).start()
    first.relay(1)

    def product(gather, g, k):
        point = (orders[k, g] if early else g) >> bits(PARTS)
        phi = jnp.dot(scaled[point], gather.whole[g], preferred_element_type=jnp.float32)
        wire = phi.astype(jnp.bfloat16)
        for r in range(row_tiles):
            for i in range(pair):
                tiles[(g * row_tiles + r) * pair + i] = (
                    wire[r * high:(r + 1) * high, i * wide:(i + 1) * wide])
        return phi

    def staged(exchange, table, plan, step):
        chunk = slot = 0
        for times, span, slots in plan.runs:
            def one(i, chunk=chunk, slot=slot, span=span, slots=slots):
                begin = chunk + i * span
                loop(begin, begin + span, step)
                exchange.part(tiles, table, slot + i * slots, slots, first=slot == 0)()
            one(0) if times == 1 else loop(0, times, one)
            chunk, slot = chunk + times * span, slot + times * slots
        loop(chunk, chunks, step)
        last = exchange.part(tiles, table, slot, capacity - slot, first=slot == 0, last=True)
        exchange.keep(tiles, table)
        last()

    def ahead_step(g):
        @pl.when(g == chunks - 3)
        def _():
            for i in range(chunks):
                second.load(i).wait()
            if early:
                second.pack(lambda i: orders[1, i])
        @pl.when(g == chunks - 1)
        def _():
            first.left(chunks - 1)
            second.start_far(0, chunks)
        @pl.when(g > 1)
        def _():
            first.relay(g)
        first.arrived(g)
        base[g] = product(first, g, 0)

    staged(ahead, item_of, ahead_plan, ahead_step)
    second.start_near(0, chunks)
    first.sent(0, chunks - 1)
    waiting = chunks // 4
    loop(0, waiting, second.relay)
    ahead.received()

    flat = landed.reshape(nboson * capacity, high, wide)
    def unpack(p):
        chi = chi_pp[pl.ds(p, 1), :]
        for c in range(col_blocks):
            for r in range(row_tiles):
                tile = flat[back_slot[(p * row_tiles + r) * col_blocks + c]]
                scaled[p, r * high:(r + 1) * high, c * wide:(c + 1) * wide] = (
                    tile.astype(jnp.float32) * chi[:, c * wide:(c + 1) * wide]).astype(jnp.bfloat16)
    loop(0, points, unpack)

    def home_step(g):
        @pl.when(g >= waiting)
        def _():
            second.relay(g)
        second.arrived(g)
        product(second, g, 1)

    staged(home, back_item_of, home_plan, home_step)
    def settle(q):
        for part in range(PARTS):
            chunk = q * PARTS + part
            at = (q, slice(None), slice(part * first.cols, (part + 1) * first.cols))
            sums[at] = gamma[at].astype(jnp.float32) + base[orders[2, chunk] if early else chunk]
    loop(0, points, settle)
    ahead.sent()
    second.sent(0, chunks)
    home.received()

    flat_back = returned.reshape(nboson * capacity, high, wide)
    def finish(q):
        for c in range(col_blocks):
            for r in range(row_tiles):
                tile = flat_back[send_slot[(q * row_tiles + r) * col_blocks + c]]
                at = (q, slice(r * high, (r + 1) * high), slice(c * wide, (c + 1) * wide))
                out[at] = (sums[at] + tile.astype(jnp.float32)).astype(jnp.bfloat16)
    loop(0, points, finish)
    home.sent()


def local(nboson, nblock, gamma_ph, full_ph, chi_ph, pp_vertex, chi_pp, relabel):
    points, rows, order = gamma_ph.shape
    row_tiles, col_blocks = relabel.shape[1] // nblock, relabel.shape[2]
    high, wide = rows // row_tiles, order // col_blocks
    total = points * row_tiles * col_blocks
    capacity = -(-total // nboson) + 1
    bf16, f32 = jnp.bfloat16, jnp.float32
    chunks, cols = points * PARTS, order // PARTS
    whole = pltpu.VMEM((chunks, order, cols), bf16)
    blocks = pltpu.VMEM((chunks, rows, cols), bf16)
    shard = pltpu.VMEM(gamma_ph.shape, bf16)
    slabs = pltpu.VMEM((nboson, capacity, high, wide), bf16)
    table_rows = -(-(nboson * capacity) // LANES) * 8
    for count in (nboson, nblock, points, row_tiles * col_blocks, col_blocks, PARTS):
        assert count & (count - 1) == 0
    vmem = pl.BlockSpec(memory_space=pltpu.VMEM)
    hbm = pl.BlockSpec(memory_space=pl.ANY)
    smem = pl.BlockSpec(memory_space=pltpu.SMEM)
    operands = (relabel.transpose(1, 2, 0), gamma_ph, full_ph, chi_ph, pp_vertex, chi_pp)

    def window(lag):
        result = pltpu.VMEM(gamma_ph.shape, bf16)
        early = lag is not None
        return pl.pallas_call(
            functools.partial(kernel, nboson, nblock, row_tiles, col_blocks, lag),
            out_shape=(result, jax.ShapeDtypeStruct((1, 1), jnp.int32)) if early else result,
            name="early" if early else "plain",
            in_specs=[hbm, hbm, hbm, vmem, hbm, vmem], out_specs=(vmem, smem) if early else vmem,
            scratch_shapes=[
                whole, whole, blocks, blocks, shard, shard, pltpu.VMEM((chunks, rows, cols), f32),
                pltpu.VMEM(gamma_ph.shape, f32),
                pltpu.VMEM((total, high, wide), bf16), slabs, slabs, slabs, slabs,
                pltpu.VMEM(operands[0].shape, jnp.int32),
                pltpu.VMEM((table_rows, LANES), jnp.int32), pltpu.SMEM((table_rows, LANES), jnp.int32),
                pltpu.VMEM((8, LANES), jnp.int32), pltpu.SMEM((8, LANES), jnp.int32),
                DMA, DMA((3,)), pltpu.SemaphoreType.REGULAR((bits(nboson),)), DMA((nboson,)), DMA((nboson,)), DMA((nboson,)), DMA((nboson,)),
            ] + gather_scratch(nblock, points) + gather_scratch(nblock, points),
            compiler_params=pltpu.CompilerParams(
                collective_id=int(early), has_side_effects=True, vmem_limit_bytes=60 * 1024 * 1024),
        )(*operands)

    if capacity <= chunks - LAG or nboson * nblock > LANES:
        return window(None)
    result, late = window(LAG)
    return lax.cond(late[0, 0] == 0, lambda: result, lambda: window(None))


def solution(mesh):
    placed = (
        P("boson", "block", None),
        P("boson", "block", None),
        P("boson", None),
        P("boson", "block", None),
        P("boson", None),
        P(),
    )
    return jax.shard_map(
        functools.partial(local, mesh.shape["boson"], mesh.shape["block"]), mesh=mesh,
        in_specs=placed, out_specs=P("boson", "block", None), check_vma=False,
    )
```
